512 devices in a mesh: prefix: 16 (over z, core), resp: 32 (over y, x).
Axes of the slice: x: 4, y: 8, z: 8, core: 2. Of those that a mesh axis runs over, the one named last changes fastest.
Arguments:
- prompt_kv: bfloat16 [2, 512, 512], P(None, 'prefix'), may hold values from -6 to 6
- response_queries: bfloat16 [1024, 128, 1792], P(('prefix', 'resp')), may hold values from -300 to 300
- resp_kv: bfloat16 [1024, 128, 512], P(('prefix', 'resp')), may hold values from -6 to 6
- readout: bfloat16 [1024, 128, 1792], P(('prefix', 'resp')), may hold values from -3 to 3
- slot_response: int32 [1024], P(('prefix', 'resp')), may hold values from 0 to 1023, each once
- lengths: int32 [1024], replicated, may hold values from 32 to 128
- pair_prompt: int32 [512], replicated, may hold values from 0 to 1
- ref_margin: float32 [512], replicated, may hold values from -60 to 60
Outputs:
- margins: float32 [512], replicated
- grad_q: bfloat16 [1024, 128, 1792], P(('prefix', 'resp'))
- grad_resp_kv: bfloat16 [1024, 128, 512], P(('prefix', 'resp'))
- grad_prompt_kv: bfloat16 [2, 512, 512], P(None, 'prefix')
The draws below stay inside these ranges and needn't reach their ends.
Inputs may be any that keep to these rules, and one draw needn't show every extreme that they name: `slot_response`: each response appears in exactly one slot; response 2 k is the chosen and 2 k + 1 the rejected response of pair k.
All inputs are finite; a program needn't handle non-finite values.
Results may differ from the reference program's by a relative error of at most 0.015.
Values may be sent and summed in bfloat16 or wider, within the bound.
No kernel may reach another device: no remote copies, remote signals or barrier semaphores. Data moves between devices by JAX's collectives and lax.ppermute only.
A program may use at most 64 MiB of HBM per device.

```python
import jax
import jax.numpy as jnp
from jax import lax

QUERY_HEADS = 14
KEY_VALUE_HEADS = 2
HEAD_SIZE = 128
RESPONSE_TOKENS = 128
PROMPT_COUNT = 2
PROMPT_TOKENS = 512
RESPONSE_COUNT = 1024
PAIRS = 512
QW = 1792
KVW = 256


def draw_response_queries(key, part):
    offset_start = jnp.clip(jax.random.normal(jax.random.fold_in(key, 11), (RESPONSE_COUNT, RESPONSE_TOKENS, QUERY_HEADS, HEAD_SIZE), jnp.float32), -6.0, 6.0)
    return offset_start.reshape(RESPONSE_COUNT, RESPONSE_TOKENS, QUERY_HEADS * HEAD_SIZE).astype(jnp.bfloat16)


def draw_prompt_kv(key, part):
    offset_start = jnp.clip(jax.random.normal(jax.random.fold_in(key, 23), (PROMPT_COUNT, PROMPT_TOKENS, 2 * KEY_VALUE_HEADS * HEAD_SIZE), jnp.float32), -6.0, 6.0)
    return offset_start.astype(jnp.bfloat16)


def plant(drawn, stream_key, least, largest):
    longest = drawn.shape.index(max(drawn.shape))
    spots = []
    for shift in (0, 1):
        where = [jax.random.randint(jax.random.fold_in(stream_key, axis), (), 0, length) for axis, length in enumerate(drawn.shape)]
        where[longest] = (where[longest] + shift) % drawn.shape[longest]
        spots.append(tuple(where))
    return drawn.at[spots[0]].set(least).at[spots[1]].set(largest)


def shard_levels(rng, extent, cuts, low, largest):
    gain = 1.0
    for axis_at, blocks in cuts:
        heights = jax.random.uniform(jax.random.fold_in(jax.random.fold_in(rng, 6), axis_at), (blocks,), jnp.float32, low / len(cuts), largest / len(cuts))
        gain = gain * jnp.repeat(jnp.exp(heights), extent[axis_at] // blocks).reshape((-1,) + (1,) * (len(extent) - 1 - axis_at))
    return gain


def noise(key, extent, width, reach, cuts=(), kind=jnp.bfloat16):
    values = width * jax.random.normal(key, extent, jnp.float32)
    if cuts:
        values = values * shard_levels(key, extent, cuts, -0.22, 0.18)
    return jnp.clip(values, -reach, reach).astype(kind)


def setup_inputs(seed: int = 0) -> dict:
    key_of = jax.random.split(jax.random.key(seed), 9)
    prompt_kv = draw_prompt_kv(jax.random.fold_in(key_of[8], 71), 0)
    response_queries = draw_response_queries(jax.random.fold_in(key_of[8], 71), 0)
    resp_kv = noise(key_of[2], (RESPONSE_COUNT, RESPONSE_TOKENS, 2 * KVW), 1.0, 6.0, ((0, 512),))
    readout = noise(key_of[3], (RESPONSE_COUNT, RESPONSE_TOKENS, QW), 0.5, 3.0, ((0, 512),))
    slot_response = jax.random.permutation(key_of[4], RESPONSE_COUNT).astype(jnp.int32)
    lengths = plant(jax.random.randint(key_of[5], (RESPONSE_COUNT,), RESPONSE_TOKENS // 4, RESPONSE_TOKENS + 1), jax.random.fold_in(key_of[5], 1), RESPONSE_TOKENS // 4, RESPONSE_TOKENS).astype(jnp.int32)
    pair_prompt = plant(jax.random.randint(key_of[6], (PAIRS,), 0, PROMPT_COUNT), jax.random.fold_in(key_of[6], 1), 0, PROMPT_COUNT - 1).astype(jnp.int32)
    ref_margin = noise(key_of[7], (PAIRS,), 10.0, 60.0, (), jnp.float32)
    return {"prompt_kv": prompt_kv, "response_queries": response_queries, "resp_kv": resp_kv, "readout": readout, "slot_response": slot_response, "lengths": lengths, "pair_prompt": pair_prompt, "ref_margin": ref_margin}


margin_beta = 0.1
loss_scale = 256.0
highest = lax.Precision.HIGHEST


def inner_product(form, left, right):
    return jnp.einsum(form, left.astype(jnp.float32), right.astype(jnp.float32), precision=highest)


def unpack(packed_rows):
    row_block = packed_rows.shape[0]
    key_rows = packed_rows[:, :KEY_VALUE_HEADS * HEAD_SIZE].reshape(row_block, KEY_VALUE_HEADS, HEAD_SIZE)
    value_rows = packed_rows[:, KEY_VALUE_HEADS * HEAD_SIZE:].reshape(row_block, KEY_VALUE_HEADS, HEAD_SIZE)
    return key_rows, value_rows


def forward_pieces(query_rows, prompt_packed, own_packed):
    prompt_keys, prompt_values = unpack(prompt_packed)
    own_keys, own_values = unpack(own_packed)
    positions = jnp.arange(RESPONSE_TOKENS)
    causal = positions[None, :] <= positions[:, None]
    scale_factor = HEAD_SIZE ** -0.5
    prompt_scores = inner_product("tgjd,kgd->gjtk", query_rows, prompt_keys) * scale_factor
    own_scores = inner_product("tgjd,kgd->gjtk", query_rows, own_keys) * scale_factor
    own_scores = jnp.where(causal, own_scores, -jnp.inf)
    row_max = jnp.maximum(jnp.max(prompt_scores, -1, keepdims=True), jnp.max(own_scores, -1, keepdims=True))
    prompt_exp = jnp.exp(prompt_scores - row_max)
    own_exp = jnp.exp(own_scores - row_max)
    total = jnp.sum(prompt_exp, -1, keepdims=True) + jnp.sum(own_exp, -1, keepdims=True)
    prefix_probabilities = (prompt_exp / total).astype(jnp.bfloat16)
    self_probabilities = (own_exp / total).astype(jnp.bfloat16)
    attended = inner_product("gjtk,kgd->tgjd", prefix_probabilities, prompt_values) + inner_product("gjtk,kgd->tgjd", self_probabilities, own_values)
    return prompt_keys, prompt_values, own_keys, own_values, prefix_probabilities, self_probabilities, attended


def reference(prompt_kv, response_queries, resp_kv, readout, slot_response, lengths, pair_prompt, ref_margin):
    query_groups = QUERY_HEADS // KEY_VALUE_HEADS
    scale_factor = HEAD_SIZE ** -0.5
    query_rows_total = response_queries.reshape(RESPONSE_COUNT, RESPONSE_TOKENS, KEY_VALUE_HEADS, query_groups, HEAD_SIZE)
    output_rows_total = readout.reshape(RESPONSE_COUNT, RESPONSE_TOKENS, KEY_VALUE_HEADS, query_groups, HEAD_SIZE)
    pair_of_slot = (slot_response // 2).astype(jnp.int32)
    sign_of_slot = 1.0 - 2.0 * (slot_response % 2).astype(jnp.float32)
    length_of_slot = lengths[slot_response]
    prompt_of_slot = pair_prompt[pair_of_slot].astype(jnp.int32)

    def slot_logp(items):
        query_rows, own_packed, output_rows, prompt, length = items
        prompt_packed = lax.dynamic_index_in_dim(prompt_kv, prompt, 0, keepdims=False)
        attended = forward_pieces(query_rows, prompt_packed, own_packed)[-1]
        valid = (jnp.arange(RESPONSE_TOKENS) < length).astype(jnp.float32)
        token_logp = jnp.sum(attended * output_rows.astype(jnp.float32), axis=(1, 2, 3)) * valid
        return jnp.sum(token_logp)

    slot_sums = lax.map(slot_logp, (query_rows_total, resp_kv, output_rows_total, prompt_of_slot, length_of_slot))
    pair_sums = jnp.zeros((PAIRS,), jnp.float32).at[pair_of_slot].add(sign_of_slot * slot_sums)
    margins = margin_beta * (pair_sums - ref_margin)
    weights = -loss_scale * margin_beta * jax.nn.sigmoid(-margins)
    coefficient_of_slot = weights[pair_of_slot] * sign_of_slot

    def slot_backward(partial_value, items):
        query_rows, own_packed, output_rows, prompt, length, coefficient = items
        prompt_packed = lax.dynamic_index_in_dim(prompt_kv, prompt, 0, keepdims=False)
        prompt_keys, prompt_values, own_keys, own_values, prefix_probabilities, self_probabilities, attended = forward_pieces(query_rows, prompt_packed, own_packed)
        valid = (jnp.arange(RESPONSE_TOKENS) < length).astype(jnp.float32)
        output_gradient = (coefficient * output_rows.astype(jnp.float32) * valid[:, None, None, None]).astype(jnp.bfloat16)
        prompt_dprobs = inner_product("tgjd,kgd->gjtk", output_gradient, prompt_values)
        own_dprobs = inner_product("tgjd,kgd->gjtk", output_gradient, own_values)
        delta = jnp.transpose(jnp.sum(output_gradient.astype(jnp.float32) * attended, -1), (1, 2, 0))[..., None]
        prefix_score_gradient = (prefix_probabilities.astype(jnp.float32) * (prompt_dprobs - delta) * scale_factor).astype(jnp.bfloat16)
        self_score_gradient = (self_probabilities.astype(jnp.float32) * (own_dprobs - delta) * scale_factor).astype(jnp.bfloat16)
        grad_queries = inner_product("gjtk,kgd->tgjd", prefix_score_gradient, prompt_keys) + inner_product("gjtk,kgd->tgjd", self_score_gradient, own_keys)
        prompt_grad = jnp.concatenate([
            inner_product("hybi,bhyu->ihu", prefix_score_gradient, query_rows).reshape(PROMPT_TOKENS, KEY_VALUE_HEADS * HEAD_SIZE),
            inner_product("hybi,bhyu->ihu", prefix_probabilities, output_gradient).reshape(PROMPT_TOKENS, KEY_VALUE_HEADS * HEAD_SIZE)], axis=-1)
        own_grad = jnp.concatenate([
            inner_product("hybi,bhyu->ihu", self_score_gradient, query_rows).reshape(RESPONSE_TOKENS, KEY_VALUE_HEADS * HEAD_SIZE),
            inner_product("hybi,bhyu->ihu", self_probabilities, output_gradient).reshape(RESPONSE_TOKENS, KEY_VALUE_HEADS * HEAD_SIZE)], axis=-1)
        selector = (jnp.arange(PROMPT_COUNT) == prompt)[:, None, None]
        partial_value = partial_value + jnp.where(selector, prompt_grad[None], 0.0)
        return partial_value, (grad_queries.reshape(RESPONSE_TOKENS, QUERY_HEADS * HEAD_SIZE).astype(jnp.bfloat16), own_grad.astype(jnp.bfloat16))

    begin_offset = jnp.zeros((PROMPT_COUNT, PROMPT_TOKENS, 2 * KEY_VALUE_HEADS * HEAD_SIZE), jnp.float32)
    partial_value, outputs = lax.scan(slot_backward, begin_offset, (query_rows_total, resp_kv, output_rows_total, prompt_of_slot, length_of_slot, coefficient_of_slot))
    grad_q, grad_resp_kv = outputs
    return margins, grad_q, grad_resp_kv, partial_value.astype(jnp.bfloat16)
```

```python
import functools
import math

import jax
import jax.numpy as jnp
from jax import lax
from jax.experimental import pallas as pl
from jax.experimental.pallas import tpu as pltpu
from jax.sharding import Mesh
from jax.sharding import PartitionSpec as P

QUERY_HEADS = 14
KEY_VALUE_HEADS = 2
HEAD = 128
GROUP = QUERY_HEADS // KEY_VALUE_HEADS
TOKENS = 128
SCALE = HEAD**-0.5
LOG2_SCALE = SCALE * math.log2(math.e)
MARGIN_BETA = 0.1
LOSS_SCALE = 256.0
PREFIX = ("z", "c")
RESP = ("y", "x")
EVERY = ("z", "c", "y", "x")
SPREAD = ("z", "c", "y")
NT = (((1,), (1,)), ((), ()))
NN = (((1,), (0,)), ((), ()))
bf16 = jnp.bfloat16
f32 = jnp.float32


def attention_kernel(
    response_ref, lengths_ref, pair_prompt_ref, place_ref,
    q_ref, r_ref, own_ref, near_ref, far_ref,
    dq_ref, down_ref, spread_ref, contrib_ref,
    key_s, value_s, probs_s, dscores_s, q_s, r_s, sums_s,
):
    slot = pl.program_id(0)
    group = pl.program_id(1)
    response = response_ref[slot]
    length = lengths_ref[response]
    prompt = pair_prompt_ref[response // 2]
    mine = place_ref[0]
    column = pl.multiple_of(group * HEAD, HEAD)
    for dest, base in ((key_s, 0), (value_s, KEY_VALUE_HEADS * HEAD)):
        at = pl.ds(pl.multiple_of(base + column, HEAD), HEAD)
        dest[0:256, :] = near_ref[:, prompt, :, at].reshape(256, HEAD)
        dest[256:512, :] = far_ref[:, prompt, :, at].reshape(256, HEAD)
        dest[512:640, :] = own_ref[0, :, at]
    key = key_s[...]
    value = value_s[...]
    live = lax.broadcasted_iota(jnp.int32, (TOKENS, HEAD), 0) < length
    for h in range(GROUP):
        rows = slice(h * TOKENS, (h + 1) * TOKENS)
        columns = slice(h * HEAD, (h + 1) * HEAD)
        q_s[rows, :] = q_ref[0, :, columns]
        r_s[rows, :] = jnp.where(live, r_ref[0, :, columns], jnp.zeros((), bf16))
    total = jnp.zeros((1, TOKENS), f32)
    start = 0
    for heads in (2, 2, 2, 1):
        n = heads * TOKENS
        rows = slice(start * TOKENS, start * TOKENS + n)
        scores = lax.dot_general(key, q_s[rows, :], NT, preferred_element_type=f32)
        dprobs = lax.dot_general(value, r_s[rows, :], NT, preferred_element_type=f32)
        j = lax.broadcasted_iota(jnp.int32, (TOKENS, n), 0)
        t = lax.broadcasted_iota(jnp.int32, (TOKENS, n), 1) % TOKENS
        scores = jnp.concatenate(
            [scores[:512], jnp.where(j <= t, scores[512:], -1e30)], axis=0
        )
        top = jnp.max(scores, axis=0, keepdims=True)
        weight = jnp.exp2((scores - top) * LOG2_SCALE)
        probs = weight * (1.0 / jnp.sum(weight, axis=0, keepdims=True))
        delta = jnp.sum(probs * dprobs, axis=0, keepdims=True)
        probs_s[:, rows] = probs.astype(bf16)
        dscores_s[:, rows] = (probs * (dprobs - delta)).astype(bf16)
        for h in range(heads):
            total = total + delta[:, h * TOKENS : (h + 1) * TOKENS]
        start += heads
    dkey = lax.dot_general(dscores_s[...], q_s[...], NN, preferred_element_type=f32) * SCALE
    dvalue = lax.dot_general(probs_s[...], r_s[...], NN, preferred_element_type=f32)
    dq = lax.dot_general(key.T, dscores_s[...], NN, preferred_element_type=f32) * SCALE
    for h in range(GROUP):
        part = slice(h * HEAD, (h + 1) * HEAD)
        dq_ref[0, :, part] = dq[:, part].T.astype(bf16)
    for i, grad in enumerate((dkey, dvalue)):
        grad = grad.astype(bf16)
        base = i * KEY_VALUE_HEADS * HEAD
        down_ref[0, :, pl.ds(pl.multiple_of(base + column, HEAD), HEAD)] = grad[512:]
        pieces = grad[:512].reshape(2, 8, 2, 16, HEAD)
        for core in range(2):
            for half in range(2):
                piece = half * 4 + i * KEY_VALUE_HEADS + group
                spread_ref[:, jnp.bitwise_xor(mine, core), piece, slot] = pieces[core, :, half]
    total = jnp.sum(total, axis=1, keepdims=True)

    @pl.when(group == 0)
    def _():
        sums_s[slot] = jnp.broadcast_to(total, (8, HEAD))

    @pl.when(group == 1)
    def _():
        sums_s[slot] = sums_s[slot] + total

    @pl.when((slot == 1) & (group == 1))
    def _():
        ids = lax.broadcasted_iota(jnp.int32, (4, HEAD), 0) * HEAD
        ids = ids + lax.broadcasted_iota(jnp.int32, (4, HEAD), 1)
        contrib = jnp.zeros((4, HEAD), f32)
        for s in range(2):
            response = response_ref[s]
            sign = (1 - 2 * (response % 2)).astype(f32)
            contrib = contrib + jnp.where(ids == response // 2, sign * sums_s[s][0:4], 0.0)
        contrib_ref[...] = jnp.broadcast_to(contrib[None], contrib_ref.shape)


def attention(slot_response, lengths, pair_prompt, place, queries, readout, own, near, far):
    return pl.pallas_call(
        attention_kernel,
        out_shape=(
            jax.ShapeDtypeStruct((2, TOKENS, QUERY_HEADS * HEAD), bf16),
            jax.ShapeDtypeStruct((2, TOKENS, 512), bf16),
            jax.ShapeDtypeStruct((8, 2, 8, 2, 16, HEAD), bf16),
            jax.ShapeDtypeStruct((64, 4, HEAD), f32),
        ),
        grid_spec=pltpu.PrefetchScalarGridSpec(
            num_scalar_prefetch=4,
            grid=(2, 2),
            in_specs=[
                pl.BlockSpec((1, TOKENS, GROUP * HEAD), lambda s, g, *_: (s, 0, g)),
                pl.BlockSpec((1, TOKENS, GROUP * HEAD), lambda s, g, *_: (s, 0, g)),
                pl.BlockSpec((1, TOKENS, 512), lambda s, g, *_: (s, 0, 0)),
                pl.BlockSpec((8, 2, 32, 512), lambda s, g, *_: (0, 0, 0, 0)),
                pl.BlockSpec((8, 2, 32, 512), lambda s, g, *_: (0, 0, 0, 0)),
            ],
            out_specs=[
                pl.BlockSpec((1, TOKENS, GROUP * HEAD), lambda s, g, *_: (s, 0, g)),
                pl.BlockSpec((1, TOKENS, 512), lambda s, g, *_: (s, 0, 0)),
                pl.BlockSpec((8, 2, 8, 2, 16, HEAD), lambda s, g, *_: (0, 0, 0, 0, 0, 0)),
                pl.BlockSpec((64, 4, HEAD), lambda s, g, *_: (0, 0, 0)),
            ],
            scratch_shapes=[
                pltpu.VMEM((640, HEAD), bf16),
                pltpu.VMEM((640, HEAD), bf16),
                pltpu.VMEM((640, GROUP * TOKENS), bf16),
                pltpu.VMEM((640, GROUP * TOKENS), bf16),
                pltpu.VMEM((GROUP * TOKENS, HEAD), bf16),
                pltpu.VMEM((GROUP * TOKENS, HEAD), bf16),
                pltpu.VMEM((2, 8, HEAD), f32),
            ],
        ),
        compiler_params=pltpu.CompilerParams(vmem_limit_bytes=40 << 20),
        cost_estimate=pl.CostEstimate(
            flops=3_000_000_000, bytes_accessed=6_000_000, transcendentals=2_300_000
        ),
        name="attention",
    )(slot_response, lengths, pair_prompt, place, queries, readout, own, near, far)


def weigh_kernel(weights_ref, pieces_ref, out_ref):
    def step(i, sums):
        sums = list(sums)
        for k in range(4):
            piece = pieces_ref[i * 4 + k].astype(f32)
            for p in range(2):
                sums[k % 2 * 2 + p] += weights_ref[p, i * 4 + k] * piece
        return tuple(sums)

    zero = jnp.zeros((16, HEAD), f32)
    sums = lax.fori_loop(0, pieces_ref.shape[0] // 4, step, (zero,) * 4)
    both = jnp.stack([sums[0] + sums[2], sums[1] + sums[3]]).astype(bf16)
    out_ref[...] = jnp.broadcast_to(both[None], out_ref.shape)


def weigh(weights, pieces):
    return pl.pallas_call(
        weigh_kernel,
        out_shape=jax.ShapeDtypeStruct((32, 2, 16, HEAD), bf16),
        in_specs=[
            pl.BlockSpec(memory_space=pltpu.SMEM),
            pl.BlockSpec(memory_space=pltpu.VMEM),
        ],
        out_specs=pl.BlockSpec(memory_space=pltpu.VMEM),
        name="weigh",
    )(weights, pieces)


def to_all(pieces, axes):
    return lax.all_to_all(pieces, axes, 0, 0, tiled=True)


def copies(shard, axes):
    size = lax.axis_size(axes)
    return to_all(jnp.broadcast_to(shard[None], (size, *shard.shape)), axes)


def looked_up(table, ids):
    pairs = jnp.arange(table.shape[-1])
    return jnp.sum(jnp.where(ids[..., None] == pairs, table, 0.0), axis=-1)


def on_device(
    prompt_kv, response_queries, resp_kv, readout, slot_response, lengths, pair_prompt, ref_margin
):
    near = copies(prompt_kv, "z")
    far = lax.ppermute(near, "c", [(0, 1), (1, 0)])
    place = lax.axis_index("c").astype(jnp.int32)[None]
    sources = copies(slot_response[None, :], SPREAD).reshape(-1)
    dq, down, spread, contrib = attention(
        slot_response, lengths, pair_prompt, place,
        response_queries, readout, resp_kv, near, far,
    )
    pieces = to_all(spread.reshape(128, 2, 16, HEAD), SPREAD)
    some = jnp.sum(to_all(contrib, ("z", "y")), axis=0)
    pair_sums = jnp.sum(copies(some, ("c", "x")), axis=0).reshape(-1)
    margins = MARGIN_BETA * (pair_sums - ref_margin)
    pair_weight = -LOSS_SCALE * MARGIN_BETA * jax.nn.sigmoid(-margins)

    def coefficient(response):
        sign = 1.0 - 2.0 * (response % 2).astype(f32)
        return looked_up(pair_weight, response // 2) * sign

    prompts = jnp.arange(2)[:, None]
    per_prompt = jnp.where(pair_prompt[None, :] == prompts, pair_weight[None, :], 0.0)
    sign = 1.0 - 2.0 * (sources % 2).astype(f32)
    weights = looked_up(per_prompt[:, None, :], (sources // 2)[None, :]) * sign
    own = coefficient(slot_response)[:, None, None]
    grad_q = (own * dq.astype(f32)).astype(bf16)
    grad_own = (own * down.astype(f32)).astype(bf16)
    parts = to_all(weigh(weights, pieces.reshape(256, 16, HEAD)), RESP)
    parts = jnp.sum(parts.reshape(2, 4, 4, 2, 16, HEAD).astype(f32), axis=2)
    grad_prompt = jnp.transpose(parts, (2, 0, 3, 1, 4)).reshape(2, 32, 512).astype(bf16)
    return margins, grad_q, grad_own, grad_prompt


def solution(mesh):
    split = Mesh(mesh.devices.reshape(8, 2, 8, 4), EVERY)
    in_specs = (
        P(None, PREFIX, None),
        P(EVERY, None, None),
        P(EVERY, None, None),
        P(EVERY, None, None),
        P(EVERY),
        P(),
        P(),
        P(),
    )
    out_specs = (P(), P(EVERY, None, None), P(EVERY, None, None), P(None, PREFIX, None))
    return jax.shard_map(
        on_device, mesh=split, in_specs=in_specs, out_specs=out_specs, check_vma=False
    )
```

```python
import math

import jax
import jax.numpy as jnp
from jax import lax
from jax.experimental import pallas as pl
from jax.experimental.pallas import tpu as pltpu
from jax.sharding import Mesh
from jax.sharding import PartitionSpec as P

QUERY_HEADS = 14
KEY_VALUE_HEADS = 2
HEAD = 128
GROUP = QUERY_HEADS // KEY_VALUE_HEADS
TOKENS = 128
WIDTH = GROUP * HEAD
KEYS = 640
SCALE = HEAD**-0.5
LOG2_SCALE = SCALE * math.log2(math.e)
MARGIN_BETA = 0.1
LOSS_SCALE = 256.0
EVERY = ("z", "c", "yh", "yl", "x")
PREFIX = ("z", "c")
RESP = ("yh", "yl", "x")
CLOSE = ("c", "yl", "x")
APART = ("z", "yh")
LOAD_ROWS = 272
NT = (((1,), (1,)), ((), ()))
NN = (((1,), (0,)), ((), ()))
bf16 = jnp.bfloat16
f32 = jnp.float32


def pair_grid():
    ids = lax.broadcasted_iota(jnp.int32, (4, HEAD), 0) * HEAD
    return ids + lax.broadcasted_iota(jnp.int32, (4, HEAD), 1)


def fill(dest, near_ref, far_ref, own_ref, prompt, column):
    at = pl.ds(pl.multiple_of(column, HEAD), HEAD)
    dest[0:256, :] = near_ref[:, prompt, :, at].reshape(256, HEAD)
    dest[256:512, :] = far_ref[:, prompt, :, at].reshape(256, HEAD)
    dest[512:640, :] = own_ref[0, :, at]


def stack(q_ref, r_ref, q_s, r_s, length):
    live = lax.broadcasted_iota(jnp.int32, (TOKENS, HEAD), 0) < length
    for h in range(GROUP):
        rows = slice(h * TOKENS, (h + 1) * TOKENS)
        columns = slice(h * HEAD, (h + 1) * HEAD)
        q_s[rows, :] = q_ref[0, :, columns]
        r_s[rows, :] = jnp.where(live, r_ref[0, :, columns], jnp.zeros((), bf16))


def forward_kernel(
    response_ref, lengths_ref, pair_prompt_ref,
    q_ref, r_ref, own_ref, near_ref, far_ref,
    probs_ref, dscores_ref, contrib_ref,
    key_s, value_s, q_s, r_s, sums_s,
):
    slot = pl.program_id(0)
    group = pl.program_id(1)
    response = response_ref[slot]
    prompt = pair_prompt_ref[response // 2]
    fill(key_s, near_ref, far_ref, own_ref, prompt, group * HEAD)
    fill(value_s, near_ref, far_ref, own_ref, prompt, (KEY_VALUE_HEADS + group) * HEAD)
    key = key_s[...]
    value = value_s[...]
    stack(q_ref, r_ref, q_s, r_s, lengths_ref[response])
    total = jnp.zeros((1, TOKENS), f32)
    start = 0
    for heads in (2, 2, 2, 1):
        n = heads * TOKENS
        rows = slice(start * TOKENS, start * TOKENS + n)
        scores = lax.dot_general(key, q_s[rows, :], NT, preferred_element_type=f32)
        dprobs = lax.dot_general(value, r_s[rows, :], NT, preferred_element_type=f32)
        j = lax.broadcasted_iota(jnp.int32, (TOKENS, n), 0)
        t = lax.broadcasted_iota(jnp.int32, (TOKENS, n), 1) % TOKENS
        scores = jnp.concatenate(
            [scores[:512], jnp.where(j <= t, scores[512:], -1e30)], axis=0
        )
        top = jnp.max(scores, axis=0, keepdims=True)
        weight = jnp.exp2((scores - top) * LOG2_SCALE)
        probs = weight * (1.0 / jnp.sum(weight, axis=0, keepdims=True))
        delta = jnp.sum(probs * dprobs, axis=0, keepdims=True)
        probs_ref[0, :, rows] = probs.astype(bf16)
        dscores_ref[0, :, rows] = (probs * (dprobs - delta)).astype(bf16)
        for h in range(heads):
            total = total + delta[:, h * TOKENS : (h + 1) * TOKENS]
        start += heads
    total = jnp.sum(total, axis=1, keepdims=True)

    @pl.when(group == 0)
    def _():
        sums_s[slot] = jnp.broadcast_to(total, (8, HEAD))

    @pl.when(group == 1)
    def _():
        sums_s[slot] = sums_s[slot] + total

    @pl.when((slot == 1) & (group == 1))
    def _():
        ids = pair_grid()
        contrib = jnp.zeros((4, HEAD), f32)
        for s in range(2):
            response = response_ref[s]
            sign = (1 - 2 * (response % 2)).astype(f32)
            contrib = contrib + jnp.where(ids == response // 2, sign * sums_s[s][0:4], 0.0)
        contrib_ref[...] = jnp.broadcast_to(contrib[None], contrib_ref.shape)


def backward_kernel(
    response_ref, lengths_ref, pair_prompt_ref, place_ref,
    probs_ref, dscores_ref, q_ref, r_ref, own_ref, near_ref, far_ref,
    dq_ref, down_ref, load_ref,
    key_s, q_s, r_s,
):
    slot = pl.program_id(0)
    group = pl.program_id(1)
    response = response_ref[slot]
    prompt = pair_prompt_ref[response // 2]
    mine = place_ref[0]
    fill(key_s, near_ref, far_ref, own_ref, prompt, group * HEAD)
    stack(q_ref, r_ref, q_s, r_s, lengths_ref[response])
    dscores = dscores_ref[0]
    dkey = lax.dot_general(dscores, q_s[...], NN, preferred_element_type=f32) * SCALE
    dvalue = lax.dot_general(probs_ref[0], r_s[...], NN, preferred_element_type=f32)
    dq = lax.dot_general(key_s[...].T, dscores, NN, preferred_element_type=f32) * SCALE
    for h in range(GROUP):
        part = slice(h * HEAD, (h + 1) * HEAD)
        dq_ref[0, :, part] = dq[:, part].T.astype(bf16)
    for i, grad in enumerate((dkey, dvalue)):
        grad = grad.astype(bf16)
        part = i * KEY_VALUE_HEADS + group
        down_ref[0, :, pl.ds(pl.multiple_of(part * HEAD, HEAD), HEAD)] = grad[512:]
        pieces = grad[:512].reshape(2, 8, 2, 16, HEAD)
        rows = pl.ds(pl.multiple_of(slot * 128, 128), 128)
        for core in range(2):
            for half in range(2):
                dest = jnp.bitwise_xor(mine, core) * 8 + half * 4 + part
                load_ref[dest, rows, :] = pieces[core, :, half].reshape(128, HEAD)


def whole(shape):
    return pl.BlockSpec(shape, lambda s, g, *_: (0,) * len(shape))


def by_slot(shape):
    return pl.BlockSpec(shape, lambda s, g, *_: (s, 0, 0))


def by_group(shape):
    return pl.BlockSpec(shape, lambda s, g, *_: (s, 0, g))


def by_both(shape):
    return pl.BlockSpec(shape, lambda s, g, *_: (s * 2 + g, 0, 0))


def forward(slot_response, lengths, pair_prompt, queries, readout, own, near, far):
    return pl.pallas_call(
        forward_kernel,
        out_shape=(
            jax.ShapeDtypeStruct((4, KEYS, WIDTH), bf16),
            jax.ShapeDtypeStruct((4, KEYS, WIDTH), bf16),
            jax.ShapeDtypeStruct((32, 4, HEAD), f32),
        ),
        grid_spec=pltpu.PrefetchScalarGridSpec(
            num_scalar_prefetch=3,
            grid=(2, 2),
            in_specs=[
                by_group((1, TOKENS, WIDTH)),
                by_group((1, TOKENS, WIDTH)),
                by_slot((1, TOKENS, 512)),
                whole((8, 2, 32, 512)),
                whole((8, 2, 32, 512)),
            ],
            out_specs=[
                by_both((1, KEYS, WIDTH)),
                by_both((1, KEYS, WIDTH)),
                whole((32, 4, HEAD)),
            ],
            scratch_shapes=[
                pltpu.VMEM((KEYS, HEAD), bf16),
                pltpu.VMEM((KEYS, HEAD), bf16),
                pltpu.VMEM((WIDTH, HEAD), bf16),
                pltpu.VMEM((WIDTH, HEAD), bf16),
                pltpu.VMEM((2, 8, HEAD), f32),
            ],
        ),
        compiler_params=pltpu.CompilerParams(vmem_limit_bytes=58 << 20),
        cost_estimate=pl.CostEstimate(
            flops=1_200_000_000, bytes_accessed=12_000_000, transcendentals=2_300_000
        ),
        name="forward",
    )(slot_response, lengths, pair_prompt, queries, readout, own, near, far)


def backward(
    slot_response, lengths, pair_prompt, place, probs, dscores, queries, readout, own, near, far
):
    return pl.pallas_call(
        backward_kernel,
        out_shape=(
            jax.ShapeDtypeStruct((2, TOKENS, QUERY_HEADS * HEAD), bf16),
            jax.ShapeDtypeStruct((2, TOKENS, 512), bf16),
            jax.ShapeDtypeStruct((16, LOAD_ROWS, HEAD), bf16),
        ),
        grid_spec=pltpu.PrefetchScalarGridSpec(
            num_scalar_prefetch=4,
            grid=(2, 2),
            in_specs=[
                by_both((1, KEYS, WIDTH)),
                by_both((1, KEYS, WIDTH)),
                by_group((1, TOKENS, WIDTH)),
                by_group((1, TOKENS, WIDTH)),
                by_slot((1, TOKENS, 512)),
                whole((8, 2, 32, 512)),
                whole((8, 2, 32, 512)),
            ],
            out_specs=[
                by_group((1, TOKENS, WIDTH)),
                by_slot((1, TOKENS, 512)),
                whole((16, LOAD_ROWS, HEAD)),
            ],
            scratch_shapes=[
                pltpu.VMEM((KEYS, HEAD), bf16),
                pltpu.VMEM((WIDTH, HEAD), bf16),
                pltpu.VMEM((WIDTH, HEAD), bf16),
            ],
        ),
        compiler_params=pltpu.CompilerParams(vmem_limit_bytes=58 << 20),
        cost_estimate=pl.CostEstimate(
            flops=1_800_000_000, bytes_accessed=14_000_000, transcendentals=0
        ),
        name="backward",
    )(slot_response, lengths, pair_prompt, place, probs, dscores, queries, readout, own, near, far)


def news_kernel(response_ref, contribs_ref, load_ref, out_ref, news_s, sems):
    share = contribs_ref[0]
    for i in range(1, 32):
        share = share + contribs_ref[i]
    high = share.astype(bf16).astype(f32)
    middle = (share - high).astype(bf16).astype(f32)
    low = share - high - middle
    names = []
    for slot in range(2):
        response = response_ref[slot]
        for part in (response // 32, response % 32):
            names.append(jnp.full((1, HEAD), part.astype(f32)))
    news_s[...] = jnp.concatenate([high, middle, low, *names], axis=0).astype(bf16)
    copies = [
        pltpu.make_async_copy(news_s, out_ref.at[i, 256:272], sems.at[i]) for i in range(16)
    ]
    for copy in copies:
        copy.start()
    for copy in copies:
        copy.wait()


def with_news(slot_response, contribs, load):
    return pl.pallas_call(
        news_kernel,
        out_shape=jax.ShapeDtypeStruct(load.shape, bf16),
        in_specs=[
            pl.BlockSpec(memory_space=pltpu.SMEM),
            pl.BlockSpec(memory_space=pltpu.VMEM),
            pl.BlockSpec(memory_space=pltpu.HBM),
        ],
        out_specs=pl.BlockSpec(memory_space=pltpu.HBM),
        scratch_shapes=[pltpu.VMEM((16, HEAD), bf16), pltpu.SemaphoreType.DMA((16,))],
        input_output_aliases={2: 0},
        compiler_params=pltpu.CompilerParams(vmem_limit_bytes=58 << 20),
        name="news",
    )(slot_response, contribs, load)


def weigh_kernel(ref_margin_ref, pair_prompt_ref, load_ref, margins_ref, weights_ref, out_ref, factor_s):
    pair_sums = jnp.zeros((4, HEAD), f32)
    names = []
    for source in range(16):
        n = load_ref[source, 256:272, :].astype(f32)
        pair_sums = pair_sums + (n[0:4] + n[4:8] + n[8:12])
        names += [n[12:13] * 32.0 + n[13:14], n[14:15] * 32.0 + n[15:16]]
    margins = MARGIN_BETA * (pair_sums - ref_margin_ref[...])
    margins_ref[...] = margins
    weights = -LOSS_SCALE * MARGIN_BETA * jax.nn.sigmoid(-margins)
    weights_ref[...] = weights
    responses = jnp.concatenate(names, axis=0).astype(jnp.int32)
    sign = (1 - 2 * (responses % 2)).astype(f32)
    lane = lax.broadcasted_iota(jnp.int32, (32, HEAD), 1)
    for p in range(2):
        table = jnp.where(pair_prompt_ref[...] == p, weights, 0.0)
        found = jnp.zeros((32, HEAD), f32)
        for k in range(4):
            found = jnp.where(responses // 2 == lane + k * HEAD, table[k : k + 1], found)
        factor_s[p] = sign * jnp.sum(found, axis=1, keepdims=True)

    def step(z, _):
        sums = [jnp.zeros((16, HEAD), f32) for _ in range(2)]
        for source in range(16):
            for slot in range(2):
                rows = pl.ds(pl.multiple_of(slot * 128 + z * 16, 16), 16)
                piece = load_ref[source, rows, :].astype(f32)
                at = source * 2 + slot
                for p in range(2):
                    sums[p] = sums[p] + factor_s[p, at : at + 1, :] * piece
        for p in range(2):
            out_ref[z, :, p] = sums[p].reshape(4, 4, HEAD).astype(bf16)
        return 0

    lax.fori_loop(0, 8, step, 0)


def weigh(ref_margin, pair_prompt, load):
    vmem = pl.BlockSpec(memory_space=pltpu.VMEM)
    return pl.pallas_call(
        weigh_kernel,
        out_shape=(
            jax.ShapeDtypeStruct((4, HEAD), f32),
            jax.ShapeDtypeStruct((4, HEAD), f32),
            jax.ShapeDtypeStruct((8, 4, 2, 4, HEAD), bf16),
        ),
        in_specs=[vmem, vmem, vmem],
        out_specs=(vmem, vmem, vmem),
        scratch_shapes=[pltpu.VMEM((2, 32, HEAD), f32)],
        compiler_params=pltpu.CompilerParams(vmem_limit_bytes=8 << 20),
        name="weigh",
    )(ref_margin, pair_prompt, load)


def join_kernel(parts_ref, out_ref):
    total = parts_ref[0].astype(f32)
    for i in range(1, 32):
        total = total + parts_ref[i].astype(f32)
    out_ref[...] = jnp.broadcast_to(total.astype(bf16)[None], out_ref.shape)


def join(parts):
    vmem = pl.BlockSpec(memory_space=pltpu.VMEM)
    return pl.pallas_call(
        join_kernel,
        out_shape=jax.ShapeDtypeStruct((32, 8, HEAD), bf16),
        in_specs=[vmem],
        out_specs=vmem,
        compiler_params=pltpu.CompilerParams(vmem_limit_bytes=8 << 20),
        name="join",
    )(parts)


def to_all(pieces, axes):
    return lax.all_to_all(pieces, axes, 0, 0, tiled=True)


def copies_to_all(shard, axes):
    size = lax.axis_size(axes)
    return to_all(jnp.broadcast_to(shard[None], (size, *shard.shape)), axes)


def on_device(
    prompt_kv, response_queries, resp_kv, readout, slot_response, lengths, pair_prompt, ref_margin
):
    near = copies_to_all(prompt_kv, "z")
    far = lax.ppermute(near, "c", [(0, 1), (1, 0)])
    place = lax.axis_index("c").astype(jnp.int32)[None]
    data = (response_queries, readout, resp_kv, near, far)
    probs, dscores, contrib = forward(slot_response, lengths, pair_prompt, *data)
    contribs = to_all(contrib, APART)
    dq, down, load = backward(
        slot_response, lengths, pair_prompt, place, probs, dscores, *data
    )
    load = to_all(with_news(slot_response, contribs, load), CLOSE)
    margins, weights, parts = weigh(
        ref_margin.reshape(4, HEAD), pair_prompt.reshape(4, HEAD), load
    )
    pairs = jnp.arange(ref_margin.shape[0])
    sign = 1.0 - 2.0 * (slot_response % 2).astype(f32)
    found = jnp.where((slot_response // 2)[:, None] == pairs, weights.reshape(1, -1), 0.0)
    own = (jnp.sum(found, axis=1) * sign)[:, None, None]
    grad_q = (own * dq.astype(f32)).astype(bf16)
    grad_own = (own * down.astype(f32)).astype(bf16)
    total = join(to_all(parts.reshape(32, 8, HEAD), APART))
    total = to_all(total, RESP).reshape(4, 2, 4, 2, 4, HEAD)
    grad_prompt = jnp.transpose(total, (3, 1, 0, 4, 2, 5)).reshape(2, 32, 512)
    return margins.reshape(-1), grad_q, grad_own, grad_prompt


def solution(mesh):
    split = Mesh(mesh.devices.reshape(8, 2, 4, 2, 4), EVERY)
    in_specs = (
        P(None, PREFIX, None),
        P(EVERY, None, None),
        P(EVERY, None, None),
        P(EVERY, None, None),
        P(EVERY),
        P(),
        P(),
        P(),
    )
    out_specs = (P(), P(EVERY, None, None), P(EVERY, None, None), P(None, PREFIX, None))
    return jax.shard_map(
        on_device, mesh=split, in_specs=in_specs, out_specs=out_specs, check_vma=False
    )
```

```python
import math

import jax
import jax.numpy as jnp
from jax import lax
from jax.experimental import pallas as pl
from jax.experimental.pallas import tpu as pltpu
from jax.sharding import Mesh
from jax.sharding import PartitionSpec as P

QUERY_HEADS = 14
KEY_VALUE_HEADS = 2
HEAD = 128
GROUP = QUERY_HEADS // KEY_VALUE_HEADS
TOKENS = 128
WIDTH = GROUP * HEAD
KEYS = 640
SCALE = HEAD**-0.5
LOG2_SCALE = SCALE * math.log2(math.e)
MARGIN_BETA = 0.1
LOSS_SCALE = 256.0
EVERY = ("z", "c", "y", "x")
PREFIX = ("z", "c")
RESP = ("y", "x")
CLOSE = ("c", "x")
APART = ("z", "y")
LOAD_ROWS = 528
NT = (((1,), (1,)), ((), ()))
NN = (((1,), (0,)), ((), ()))
bf16 = jnp.bfloat16
f32 = jnp.float32


def pair_grid():
    ids = lax.broadcasted_iota(jnp.int32, (4, HEAD), 0) * HEAD
    return ids + lax.broadcasted_iota(jnp.int32, (4, HEAD), 1)


def fill(dest, near_ref, far_ref, own_ref, prompt, column):
    at = pl.ds(pl.multiple_of(column, HEAD), HEAD)
    dest[0:256, :] = near_ref[:, prompt, :, at].reshape(256, HEAD)
    dest[256:512, :] = far_ref[:, prompt, :, at].reshape(256, HEAD)
    dest[512:640, :] = own_ref[0, :, at]


def stack(q_ref, r_ref, q_s, r_s, length):
    live = lax.broadcasted_iota(jnp.int32, (TOKENS, HEAD), 0) < length
    for h in range(GROUP):
        rows = slice(h * TOKENS, (h + 1) * TOKENS)
        columns = slice(h * HEAD, (h + 1) * HEAD)
        q_s[rows, :] = q_ref[0, :, columns]
        r_s[rows, :] = jnp.where(live, r_ref[0, :, columns], jnp.zeros((), bf16))


def forward_kernel(
    response_ref, lengths_ref, pair_prompt_ref,
    q_ref, r_ref, own_ref, near_ref, far_ref,
    stats_ref, contrib_ref,
    key_s, value_s, q_s, r_s, sums_s,
):
    slot = pl.program_id(0)
    group = pl.program_id(1)
    response = response_ref[slot]
    prompt = pair_prompt_ref[response // 2]
    fill(key_s, near_ref, far_ref, own_ref, prompt, group * HEAD)
    fill(value_s, near_ref, far_ref, own_ref, prompt, (KEY_VALUE_HEADS + group) * HEAD)
    stack(q_ref, r_ref, q_s, r_s, lengths_ref[response])
    scores = lax.dot_general(key_s[...], q_s[...], NT, preferred_element_type=f32)
    dprobs = lax.dot_general(value_s[...], r_s[...], NT, preferred_element_type=f32)
    scores = masked(scores)
    top = jnp.max(scores, axis=0, keepdims=True)
    weight = jnp.exp2((scores - top) * LOG2_SCALE)
    share = 1.0 / jnp.sum(weight, axis=0, keepdims=True)
    delta = jnp.sum(weight * dprobs, axis=0, keepdims=True) * share
    at = slot * KEY_VALUE_HEADS + group
    stats_ref[at, 0:1, :] = top
    stats_ref[at, 1:2, :] = share
    stats_ref[at, 2:3, :] = delta
    total = jnp.sum(delta, axis=1, keepdims=True)

    @pl.when(group == 0)
    def _():
        sums_s[slot] = jnp.broadcast_to(total, (8, HEAD))

    @pl.when(group == 1)
    def _():
        sums_s[slot] = sums_s[slot] + total

    @pl.when((slot == 1) & (group == 1))
    def _():
        ids = pair_grid()
        contrib = jnp.zeros((4, HEAD), f32)
        for s in range(2):
            response = response_ref[s]
            sign = (1 - 2 * (response % 2)).astype(f32)
            contrib = contrib + jnp.where(ids == response // 2, sign * sums_s[s][0:4], 0.0)
        contrib_ref[...] = jnp.broadcast_to(contrib[None], contrib_ref.shape)


def masked(scores):
    j = lax.broadcasted_iota(jnp.int32, (TOKENS, WIDTH), 0)
    t = lax.broadcasted_iota(jnp.int32, (TOKENS, WIDTH), 1) % TOKENS
    return jnp.concatenate([scores[:512], jnp.where(j <= t, scores[512:], -1e30)], axis=0)


def backward_kernel(
    response_ref, lengths_ref, pair_prompt_ref, place_ref,
    stats_ref, q_ref, r_ref, own_ref, near_ref, far_ref,
    dq_ref, down_ref, load_ref,
    key_s, value_s, q_s, r_s, probs_s, dscores_s,
):
    slot = pl.program_id(0)
    group = pl.program_id(1)
    response = response_ref[slot]
    prompt = pair_prompt_ref[response // 2]
    mine = place_ref[0]
    fill(key_s, near_ref, far_ref, own_ref, prompt, group * HEAD)
    fill(value_s, near_ref, far_ref, own_ref, prompt, (KEY_VALUE_HEADS + group) * HEAD)
    stack(q_ref, r_ref, q_s, r_s, lengths_ref[response])
    scores = lax.dot_general(key_s[...], q_s[...], NT, preferred_element_type=f32)
    dprobs = lax.dot_general(value_s[...], r_s[...], NT, preferred_element_type=f32)
    at = slot * KEY_VALUE_HEADS + group
    top, share, delta = (stats_ref[at, i : i + 1, :] for i in range(3))
    probs = jnp.exp2((masked(scores) - top) * LOG2_SCALE) * share
    probs_s[...] = probs.astype(bf16)
    dscores_s[...] = (probs * (dprobs - delta)).astype(bf16)
    dkey = lax.dot_general(dscores_s[...], q_s[...], NN, preferred_element_type=f32) * SCALE
    dvalue = lax.dot_general(probs_s[...], r_s[...], NN, preferred_element_type=f32)
    dq = lax.dot_general(key_s[...].T, dscores_s[...], NN, preferred_element_type=f32) * SCALE
    for h in range(GROUP):
        part = slice(h * HEAD, (h + 1) * HEAD)
        dq_ref[0, :, part] = dq[:, part].T.astype(bf16)
    for i, grad in enumerate((dkey, dvalue)):
        grad = grad.astype(bf16)
        part = i * KEY_VALUE_HEADS + group
        down_ref[0, :, pl.ds(pl.multiple_of(part * HEAD, HEAD), HEAD)] = grad[512:]
        rows = pl.ds(pl.multiple_of(slot * 256, 256), 256)
        for core in range(2):
            dest = jnp.bitwise_xor(mine, core) * 4 + part
            load_ref[dest, rows, :] = grad[core * 256 : (core + 1) * 256]


def whole(shape):
    return pl.BlockSpec(shape, lambda s, g, *_: (0,) * len(shape))


def by_slot(shape):
    return pl.BlockSpec(shape, lambda s, g, *_: (s, 0, 0))


def by_group(shape):
    return pl.BlockSpec(shape, lambda s, g, *_: (s, 0, g))


def forward(slot_response, lengths, pair_prompt, queries, readout, own, near, far):
    return pl.pallas_call(
        forward_kernel,
        out_shape=(
            jax.ShapeDtypeStruct((4, 8, WIDTH), f32),
            jax.ShapeDtypeStruct((64, 4, HEAD), f32),
        ),
        grid_spec=pltpu.PrefetchScalarGridSpec(
            num_scalar_prefetch=3,
            grid=(2, 2),
            in_specs=[
                by_group((1, TOKENS, WIDTH)),
                by_group((1, TOKENS, WIDTH)),
                by_slot((1, TOKENS, 512)),
                whole((8, 2, 32, 512)),
                whole((8, 2, 32, 512)),
            ],
            out_specs=[
                whole((4, 8, WIDTH)),
                whole((64, 4, HEAD)),
            ],
            scratch_shapes=[
                pltpu.VMEM((KEYS, HEAD), bf16),
                pltpu.VMEM((KEYS, HEAD), bf16),
                pltpu.VMEM((WIDTH, HEAD), bf16),
                pltpu.VMEM((WIDTH, HEAD), bf16),
                pltpu.VMEM((2, 8, HEAD), f32),
            ],
        ),
        compiler_params=pltpu.CompilerParams(vmem_limit_bytes=52 << 20),
        cost_estimate=pl.CostEstimate(
            flops=1_200_000_000, bytes_accessed=4_000_000, transcendentals=2_300_000
        ),
        name="forward",
    )(slot_response, lengths, pair_prompt, queries, readout, own, near, far)


def backward(
    slot_response, lengths, pair_prompt, place, stats, queries, readout, own, near, far
):
    return pl.pallas_call(
        backward_kernel,
        out_shape=(
            jax.ShapeDtypeStruct((2, TOKENS, QUERY_HEADS * HEAD), bf16),
            jax.ShapeDtypeStruct((2, TOKENS, 512), bf16),
            jax.ShapeDtypeStruct((8, LOAD_ROWS, HEAD), bf16),
        ),
        grid_spec=pltpu.PrefetchScalarGridSpec(
            num_scalar_prefetch=4,
            grid=(2, 2),
            in_specs=[
                whole((4, 8, WIDTH)),
                by_group((1, TOKENS, WIDTH)),
                by_group((1, TOKENS, WIDTH)),
                by_slot((1, TOKENS, 512)),
                whole((8, 2, 32, 512)),
                whole((8, 2, 32, 512)),
            ],
            out_specs=[
                by_group((1, TOKENS, WIDTH)),
                by_slot((1, TOKENS, 512)),
                whole((8, LOAD_ROWS, HEAD)),
            ],
            scratch_shapes=[
                pltpu.VMEM((KEYS, HEAD), bf16),
                pltpu.VMEM((KEYS, HEAD), bf16),
                pltpu.VMEM((WIDTH, HEAD), bf16),
                pltpu.VMEM((WIDTH, HEAD), bf16),
                pltpu.VMEM((KEYS, WIDTH), bf16),
                pltpu.VMEM((KEYS, WIDTH), bf16),
            ],
        ),
        compiler_params=pltpu.CompilerParams(vmem_limit_bytes=52 << 20),
        cost_estimate=pl.CostEstimate(
            flops=3_000_000_000, bytes_accessed=6_000_000, transcendentals=2_300_000
        ),
        name="backward",
    )(slot_response, lengths, pair_prompt, place, stats, queries, readout, own, near, far)


def news_kernel(response_ref, contribs_ref, load_ref, out_ref, news_s, sems):
    share = contribs_ref[0]
    for i in range(1, 64):
        share = share + contribs_ref[i]
    high = share.astype(bf16).astype(f32)
    middle = (share - high).astype(bf16).astype(f32)
    low = share - high - middle
    names = []
    for slot in range(2):
        response = response_ref[slot]
        for part in (response // 32, response % 32):
            names.append(jnp.full((1, HEAD), part.astype(f32)))
    news_s[...] = jnp.concatenate([high, middle, low, *names], axis=0).astype(bf16)
    copies = [
        pltpu.make_async_copy(news_s, out_ref.at[i, 512:528], sems.at[i]) for i in range(8)
    ]
    for copy in copies:
        copy.start()
    for copy in copies:
        copy.wait()


def with_news(slot_response, contribs, load):
    return pl.pallas_call(
        news_kernel,
        out_shape=jax.ShapeDtypeStruct(load.shape, bf16),
        in_specs=[
            pl.BlockSpec(memory_space=pltpu.SMEM),
            pl.BlockSpec(memory_space=pltpu.VMEM),
            pl.BlockSpec(memory_space=pltpu.HBM),
        ],
        out_specs=pl.BlockSpec(memory_space=pltpu.HBM),
        scratch_shapes=[pltpu.VMEM((16, HEAD), bf16), pltpu.SemaphoreType.DMA((8,))],
        input_output_aliases={2: 0},
        compiler_params=pltpu.CompilerParams(vmem_limit_bytes=58 << 20),
        name="news",
    )(slot_response, contribs, load)


def weigh_kernel(ref_margin_ref, pair_prompt_ref, load_ref, margins_ref, weights_ref, out_ref, factor_s):
    pair_sums = jnp.zeros((4, HEAD), f32)
    names = []
    for source in range(8):
        n = load_ref[source, 512:528, :].astype(f32)
        pair_sums = pair_sums + (n[0:4] + n[4:8] + n[8:12])
        names += [n[12:13] * 32.0 + n[13:14], n[14:15] * 32.0 + n[15:16]]
    margins = MARGIN_BETA * (pair_sums - ref_margin_ref[...])
    margins_ref[...] = margins
    weights = -LOSS_SCALE * MARGIN_BETA * jax.nn.sigmoid(-margins)
    weights_ref[...] = weights
    responses = jnp.concatenate(names, axis=0).astype(jnp.int32)
    sign = (1 - 2 * (responses % 2)).astype(f32)
    lane = lax.broadcasted_iota(jnp.int32, (16, HEAD), 1)
    for p in range(2):
        table = jnp.where(pair_prompt_ref[...] == p, weights, 0.0)
        found = jnp.zeros((16, HEAD), f32)
        for k in range(4):
            found = jnp.where(responses // 2 == lane + k * HEAD, table[k : k + 1], found)
        factor_s[p] = sign * jnp.sum(found, axis=1, keepdims=True)

    def step(z, _):
        sums = [jnp.zeros((32, HEAD), f32) for _ in range(2)]
        for source in range(8):
            for slot in range(2):
                rows = pl.ds(pl.multiple_of(slot * 256 + z * 32, 32), 32)
                piece = load_ref[source, rows, :].astype(f32)
                at = source * 2 + slot
                for p in range(2):
                    sums[p] = sums[p] + factor_s[p, at : at + 1, :] * piece
        for p in range(2):
            out_ref[z, :, p] = sums[p].reshape(8, 4, HEAD).astype(bf16)
        return 0

    lax.fori_loop(0, 8, step, 0)


def weigh(ref_margin, pair_prompt, load):
    vmem = pl.BlockSpec(memory_space=pltpu.VMEM)
    return pl.pallas_call(
        weigh_kernel,
        out_shape=(
            jax.ShapeDtypeStruct((4, HEAD), f32),
            jax.ShapeDtypeStruct((4, HEAD), f32),
            jax.ShapeDtypeStruct((8, 8, 2, 4, HEAD), bf16),
        ),
        in_specs=[vmem, vmem, vmem],
        out_specs=(vmem, vmem, vmem),
        scratch_shapes=[pltpu.VMEM((2, 16, HEAD), f32)],
        compiler_params=pltpu.CompilerParams(vmem_limit_bytes=8 << 20),
        name="weigh",
    )(ref_margin, pair_prompt, load)


def join_kernel(parts_ref, out_ref):
    total = parts_ref[0].astype(f32)
    for i in range(1, 64):
        total = total + parts_ref[i].astype(f32)
    out_ref[...] = jnp.broadcast_to(total.astype(bf16)[None], out_ref.shape)


def join(parts):
    vmem = pl.BlockSpec(memory_space=pltpu.VMEM)
    return pl.pallas_call(
        join_kernel,
        out_shape=jax.ShapeDtypeStruct((32, 8, HEAD), bf16),
        in_specs=[vmem],
        out_specs=vmem,
        compiler_params=pltpu.CompilerParams(vmem_limit_bytes=8 << 20),
        name="join",
    )(parts)


def to_all(pieces, axes):
    return lax.all_to_all(pieces, axes, 0, 0, tiled=True)


def copies_to_all(shard, axes):
    size = lax.axis_size(axes)
    return to_all(jnp.broadcast_to(shard[None], (size, *shard.shape)), axes)


def on_device(
    prompt_kv, response_queries, resp_kv, readout, slot_response, lengths, pair_prompt, ref_margin
):
    near = copies_to_all(prompt_kv, "z")
    far = lax.ppermute(near, "c", [(0, 1), (1, 0)])
    place = lax.axis_index("c").astype(jnp.int32)[None]
    data = (response_queries, readout, resp_kv, near, far)
    stats, contrib = forward(slot_response, lengths, pair_prompt, *data)
    contribs = to_all(contrib, APART)
    dq, down, load = backward(slot_response, lengths, pair_prompt, place, stats, *data)
    load = to_all(with_news(slot_response, contribs, load), CLOSE)
    margins, weights, parts = weigh(
        ref_margin.reshape(4, HEAD), pair_prompt.reshape(4, HEAD), load
    )
    pairs = jnp.arange(ref_margin.shape[0])
    sign = 1.0 - 2.0 * (slot_response % 2).astype(f32)
    found = jnp.where((slot_response // 2)[:, None] == pairs, weights.reshape(1, -1), 0.0)
    own = (jnp.sum(found, axis=1) * sign)[:, None, None]
    grad_q = (own * dq.astype(f32)).astype(bf16)
    grad_own = (own * down.astype(f32)).astype(bf16)
    total = join(to_all(parts.reshape(64, 8, HEAD), APART))
    total = to_all(total, RESP).reshape(8, 4, 2, 4, HEAD)
    grad_prompt = jnp.transpose(total, (2, 0, 3, 1, 4)).reshape(2, 32, 512)
    return margins.reshape(-1), grad_q, grad_own, grad_prompt


def solution(mesh):
    split = Mesh(mesh.devices.reshape(8, 2, 8, 4), EVERY)
    in_specs = (
        P(None, PREFIX, None),
        P(EVERY, None, None),
        P(EVERY, None, None),
        P(EVERY, None, None),
        P(EVERY),
        P(),
        P(),
        P(),
    )
    out_specs = (P(), P(EVERY, None, None), P(EVERY, None, None), P(None, PREFIX, None))
    return jax.shard_map(
        on_device, mesh=split, in_specs=in_specs, out_specs=out_specs, check_vma=False
    )
```

```python
import math

import jax
import jax.numpy as jnp
from jax import lax
from jax.experimental import pallas as pl
from jax.experimental.pallas import tpu as pltpu
from jax.sharding import Mesh
from jax.sharding import PartitionSpec as P

QUERY_HEADS = 14
KEY_VALUE_HEADS = 2
HEAD = 128
GROUP = QUERY_HEADS // KEY_VALUE_HEADS
TOKENS = 128
WIDTH = GROUP * HEAD
KEYS = 640
SCALE = HEAD**-0.5
LOG2_SCALE = SCALE * math.log2(math.e)
MARGIN_BETA = 0.1
LOSS_SCALE = 256.0
EVERY = ("z", "c", "y", "x")
PREFIX = ("z", "c")
RESP = ("y", "x")
CLOSE = ("c", "x")
APART = ("z", "y")
LOAD_ROWS = 528
GRANT = 52
NT = (((1,), (1,)), ((), ()))
NN = (((1,), (0,)), ((), ()))
bf16 = jnp.bfloat16
f32 = jnp.float32


def pair_grid():
    ids = lax.broadcasted_iota(jnp.int32, (4, HEAD), 0) * HEAD
    return ids + lax.broadcasted_iota(jnp.int32, (4, HEAD), 1)


def fill(dest, near_ref, far_ref, prompt, column):
    at = pl.ds(pl.multiple_of(column, HEAD), HEAD)
    dest[0:256, :] = near_ref[:, prompt, :, at].reshape(256, HEAD)
    dest[256:512, :] = far_ref[:, prompt, :, at].reshape(256, HEAD)


def dots(keys, values, q, r):
    scores = lax.dot_general(keys, q, NT, preferred_element_type=f32)
    return scores, lax.dot_general(values, r, NT, preferred_element_type=f32)


def causal(scores):
    j = lax.broadcasted_iota(jnp.int32, (TOKENS, WIDTH), 0)
    t = lax.broadcasted_iota(jnp.int32, (TOKENS, WIDTH), 1) % TOKENS
    return jnp.where(j <= t, scores, -1e30)


def own_part(own_ref, group, is_value):
    column = (is_value * KEY_VALUE_HEADS + group) * HEAD
    return own_ref[0, :, pl.ds(pl.multiple_of(column, HEAD), HEAD)]


def prepare_kernel(
    response_ref, lengths_ref, q_ref, r_ref, own_ref, q_out, r_out, stats_ref
):
    group = pl.program_id(1)
    length = lengths_ref[response_ref[pl.program_id(0)]]
    live = lax.broadcasted_iota(jnp.int32, (TOKENS, HEAD), 0) < length
    for h in range(GROUP):
        rows = slice(h * TOKENS, (h + 1) * TOKENS)
        columns = slice(h * HEAD, (h + 1) * HEAD)
        q_out[0, rows, :] = q_ref[0, :, columns]
        r_out[0, rows, :] = jnp.where(live, r_ref[0, :, columns], jnp.zeros((), bf16))
    scores, dprobs = dots(
        own_part(own_ref, group, 0), own_part(own_ref, group, 1), q_out[0], r_out[0]
    )
    scores = causal(scores)
    top = jnp.max(scores, axis=0, keepdims=True)
    weight = jnp.exp2((scores - top) * LOG2_SCALE)
    stats_ref[0, 0:1, :] = top
    stats_ref[0, 1:2, :] = jnp.sum(weight, axis=0, keepdims=True)
    stats_ref[0, 2:3, :] = jnp.sum(weight * dprobs, axis=0, keepdims=True)


def forward_kernel(
    response_ref, pair_prompt_ref, q_ref, r_ref, part_ref, near_ref, far_ref,
    stats_ref, contrib_ref, key_s, value_s, sums_s,
):
    slot = pl.program_id(0)
    group = pl.program_id(1)
    prompt = pair_prompt_ref[response_ref[slot] // 2]
    fill(key_s, near_ref, far_ref, prompt, group * HEAD)
    fill(value_s, near_ref, far_ref, prompt, (KEY_VALUE_HEADS + group) * HEAD)
    top, total, delta = (part_ref[0, i : i + 1, :] for i in range(3))
    for start in range(0, 512, 128):
        keys = slice(start, start + 128)
        scores, dprobs = dots(key_s[keys, :], value_s[keys, :], q_ref[0], r_ref[0])
        higher = jnp.maximum(top, jnp.max(scores, axis=0, keepdims=True))
        weight = jnp.exp2((scores - higher) * LOG2_SCALE)
        fade = jnp.exp2((top - higher) * LOG2_SCALE)
        total = total * fade + jnp.sum(weight, axis=0, keepdims=True)
        delta = delta * fade + jnp.sum(weight * dprobs, axis=0, keepdims=True)
        top = higher
    share = 1.0 / total
    delta = delta * share
    stats_ref[0, 0:1, :] = top
    stats_ref[0, 1:2, :] = share
    stats_ref[0, 2:3, :] = delta
    total = jnp.sum(delta, axis=1, keepdims=True)

    @pl.when(group == 0)
    def _():
        sums_s[slot] = jnp.broadcast_to(total, (8, HEAD))

    @pl.when(group == 1)
    def _():
        sums_s[slot] = sums_s[slot] + total

    @pl.when((slot == 1) & (group == 1))
    def _():
        ids = pair_grid()
        contrib = jnp.zeros((4, HEAD), f32)
        for s in range(2):
            response = response_ref[s]
            sign = (1 - 2 * (response % 2)).astype(f32)
            contrib = contrib + jnp.where(ids == response // 2, sign * sums_s[s][0:4], 0.0)
        contrib_ref[...] = jnp.broadcast_to(contrib[None], contrib_ref.shape)


def backward_parts(scores, dprobs, stats_ref):
    top, share, delta = (stats_ref[0, i : i + 1, :] for i in range(3))
    probs = jnp.exp2((scores - top) * LOG2_SCALE) * share
    return probs.astype(bf16), (probs * (dprobs - delta)).astype(bf16)


def backward_kernel(
    response_ref, pair_prompt_ref, place_ref, q_ref, r_ref, stats_ref, near_ref, far_ref,
    load_ref, key_s, value_s, probs_s, dscores_s,
):
    slot = pl.program_id(0)
    group = pl.program_id(1)
    prompt = pair_prompt_ref[response_ref[slot] // 2]
    mine = place_ref[0]
    fill(key_s, near_ref, far_ref, prompt, group * HEAD)
    fill(value_s, near_ref, far_ref, prompt, (KEY_VALUE_HEADS + group) * HEAD)
    scores, dprobs = dots(key_s[...], value_s[...], q_ref[0], r_ref[0])
    probs_s[...], dscores_s[...] = backward_parts(scores, dprobs, stats_ref)
    dkey = lax.dot_general(dscores_s[...], q_ref[0], NN, preferred_element_type=f32) * SCALE
    dvalue = lax.dot_general(probs_s[...], r_ref[0], NN, preferred_element_type=f32)
    rows = pl.ds(pl.multiple_of(slot * 256, 256), 256)
    for i, grad in enumerate((dkey, dvalue)):
        grad = grad.astype(bf16)
        for core in range(2):
            dest = jnp.bitwise_xor(mine, core) * 4 + i * KEY_VALUE_HEADS + group
            load_ref[dest, rows, :] = grad[core * 256 : (core + 1) * 256]


def finish_kernel(
    response_ref, pair_prompt_ref, q_ref, r_ref, stats_ref, near_ref, far_ref, own_ref,
    dq_ref, down_ref, done_ref, key_s, value_s, probs_s, dscores_s,
):
    group = pl.program_id(1)
    prompt = pair_prompt_ref[response_ref[pl.program_id(0)] // 2]
    fill(key_s, near_ref, far_ref, prompt, group * HEAD)
    fill(value_s, near_ref, far_ref, prompt, (KEY_VALUE_HEADS + group) * HEAD)
    key_s[512:640, :] = own_part(own_ref, group, 0)
    value_s[512:640, :] = own_part(own_ref, group, 1)
    scores, dprobs = dots(key_s[...], value_s[...], q_ref[0], r_ref[0])
    scores = jnp.concatenate([scores[:512], causal(scores[512:])], axis=0)
    probs, dscores_s[...] = backward_parts(scores, dprobs, stats_ref)
    probs_s[...] = probs[512:]
    dq = lax.dot_general(key_s[...].T, dscores_s[...], NN, preferred_element_type=f32) * SCALE
    for h in range(GROUP):
        part = slice(h * HEAD, (h + 1) * HEAD)
        dq_ref[0, :, part] = dq[:, part].T.astype(bf16)
    dkey = lax.dot_general(dscores_s[512:640, :], q_ref[0], NN, preferred_element_type=f32)
    dvalue = lax.dot_general(probs_s[...], r_ref[0], NN, preferred_element_type=f32)
    column = pl.multiple_of(group * HEAD, HEAD)
    down_ref[0, :, pl.ds(column, HEAD)] = (dkey * SCALE).astype(bf16)
    column = pl.multiple_of((KEY_VALUE_HEADS + group) * HEAD, HEAD)
    down_ref[0, :, pl.ds(column, HEAD)] = dvalue.astype(bf16)
    done_ref[...] = jnp.zeros((8, HEAD), f32)


def whole(shape):
    return pl.BlockSpec(shape, lambda s, g, *_: (0,) * len(shape))


def by_slot(shape):
    return pl.BlockSpec(shape, lambda s, g, *_: (s, 0, 0))


def by_group(shape):
    return pl.BlockSpec(shape, lambda s, g, *_: (s, 0, g))


def by_both(shape):
    return pl.BlockSpec(shape, lambda s, g, *_: (s * 2 + g, 0, 0))


VMEM = pl.BlockSpec(memory_space=pltpu.VMEM)
STACK = by_both((1, WIDTH, HEAD))
STATS = by_both((1, 8, WIDTH))
STACK_SHAPE = jax.ShapeDtypeStruct((4, WIDTH, HEAD), bf16)
STATS_SHAPE = jax.ShapeDtypeStruct((4, 8, WIDTH), f32)


def per_group(kernel, name, scalars, arrays, in_specs, out_specs, out_shape, scratch, flops, exps):
    return pl.pallas_call(
        kernel,
        out_shape=out_shape,
        grid_spec=pltpu.PrefetchScalarGridSpec(
            num_scalar_prefetch=len(scalars),
            grid=(2, 2),
            in_specs=in_specs,
            out_specs=out_specs,
            scratch_shapes=scratch,
        ),
        compiler_params=pltpu.CompilerParams(vmem_limit_bytes=GRANT << 20),
        cost_estimate=pl.CostEstimate(
            flops=flops, bytes_accessed=4_000_000, transcendentals=exps
        ),
        name=name,
    )(*scalars, *arrays)


def prepare(slot_response, lengths, queries, readout, own):
    return per_group(
        prepare_kernel, "prepare",
        (slot_response, lengths), (queries, readout, own),
        [by_group((1, TOKENS, WIDTH)), by_group((1, TOKENS, WIDTH)), by_slot((1, TOKENS, 512))],
        [STACK, STACK, STATS],
        (STACK_SHAPE, STACK_SHAPE, STATS_SHAPE),
        [], 240_000_000, 460_000,
    )


def forward(slot_response, pair_prompt, q, r, part, near, far):
    return per_group(
        forward_kernel, "forward",
        (slot_response, pair_prompt), (q, r, part, near, far),
        [STACK, STACK, STATS, VMEM, VMEM],
        [STATS, whole((64, 4, HEAD))],
        (STATS_SHAPE, jax.ShapeDtypeStruct((64, 4, HEAD), f32)),
        [
            pltpu.VMEM((512, HEAD), bf16),
            pltpu.VMEM((512, HEAD), bf16),
            pltpu.VMEM((2, 8, HEAD), f32),
        ],
        940_000_000, 1_800_000,
    )


def backward(slot_response, pair_prompt, place, q, r, stats, near, far):
    return per_group(
        backward_kernel, "backward",
        (slot_response, pair_prompt, place), (q, r, stats, near, far),
        [STACK, STACK, STATS, VMEM, VMEM],
        whole((8, LOAD_ROWS, HEAD)),
        jax.ShapeDtypeStruct((8, LOAD_ROWS, HEAD), bf16),
        [
            pltpu.VMEM((512, HEAD), bf16),
            pltpu.VMEM((512, HEAD), bf16),
            pltpu.VMEM((512, WIDTH), bf16),
            pltpu.VMEM((512, WIDTH), bf16),
        ],
        1_880_000_000, 1_800_000,
    )


def finish(slot_response, pair_prompt, q, r, stats, near, far, own):
    return per_group(
        finish_kernel, "finish",
        (slot_response, pair_prompt), (q, r, stats, near, far, own),
        [STACK, STACK, STATS, VMEM, VMEM, by_slot((1, TOKENS, 512))],
        [by_group((1, TOKENS, WIDTH)), by_slot((1, TOKENS, 512)), whole((8, HEAD))],
        (
            jax.ShapeDtypeStruct((2, TOKENS, QUERY_HEADS * HEAD), bf16),
            jax.ShapeDtypeStruct((2, TOKENS, 512), bf16),
            jax.ShapeDtypeStruct((8, HEAD), f32),
        ),
        [
            pltpu.VMEM((KEYS, HEAD), bf16),
            pltpu.VMEM((KEYS, HEAD), bf16),
            pltpu.VMEM((TOKENS, WIDTH), bf16),
            pltpu.VMEM((KEYS, WIDTH), bf16),
        ],
        2_000_000_000, 2_300_000,
    )


def with_news(slot_response, share, load):
    high = lax.reduce_precision(share, 8, 7)
    middle = lax.reduce_precision(share - high, 8, 7)
    low = share - high - middle
    names = jnp.stack([slot_response // 32, slot_response % 32], axis=1).reshape(4, 1)
    names = jnp.broadcast_to(names.astype(f32), (4, HEAD))
    news = jnp.concatenate([high, middle, low, names], axis=0).astype(bf16)
    news = jnp.broadcast_to(news[None], (8, 16, HEAD))
    return lax.dynamic_update_slice(load, news, (0, 512, 0))


def weigh_kernel(
    ref_margin_ref, pair_prompt_ref, load_ref, done_ref, margins_ref, weights_ref, out_ref, factor_s
):
    del done_ref
    pair_sums = jnp.zeros((4, HEAD), f32)
    names = []
    for source in range(8):
        n = load_ref[source, 512:528, :].astype(f32)
        pair_sums = pair_sums + (n[0:4] + n[4:8] + n[8:12])
        names += [n[12:13] * 32.0 + n[13:14], n[14:15] * 32.0 + n[15:16]]
    margins = MARGIN_BETA * (pair_sums - ref_margin_ref[...])
    margins_ref[...] = margins
    weights = -LOSS_SCALE * MARGIN_BETA * jax.nn.sigmoid(-margins)
    weights_ref[...] = weights
    responses = jnp.concatenate(names, axis=0).astype(jnp.int32)
    sign = (1 - 2 * (responses % 2)).astype(f32)
    lane = lax.broadcasted_iota(jnp.int32, (16, HEAD), 1)
    for p in range(2):
        table = jnp.where(pair_prompt_ref[...] == p, weights, 0.0)
        found = jnp.zeros((16, HEAD), f32)
        for k in range(4):
            found = jnp.where(responses // 2 == lane + k * HEAD, table[k : k + 1], found)
        factor_s[p] = sign * jnp.sum(found, axis=1, keepdims=True)

    def step(z, _):
        sums = [jnp.zeros((32, HEAD), f32) for _ in range(2)]
        for source in range(8):
            for slot in range(2):
                rows = pl.ds(pl.multiple_of(slot * 256 + z * 32, 32), 32)
                piece = load_ref[source, rows, :].astype(f32)
                at = source * 2 + slot
                for p in range(2):
                    sums[p] = sums[p] + factor_s[p, at : at + 1, :] * piece
        both = jnp.concatenate([s.reshape(8, 1, 4, HEAD) for s in sums], axis=1)
        out_ref[z] = both.reshape(8, 8, HEAD).astype(bf16)
        return 0

    lax.fori_loop(0, 8, step, 0)


def weigh(ref_margin, pair_prompt, load, done):
    vmem = pl.BlockSpec(memory_space=pltpu.VMEM)
    return pl.pallas_call(
        weigh_kernel,
        out_shape=(
            jax.ShapeDtypeStruct((4, HEAD), f32),
            jax.ShapeDtypeStruct((4, HEAD), f32),
            jax.ShapeDtypeStruct((8, 8, 8, HEAD), bf16),
        ),
        in_specs=[vmem, vmem, vmem, pl.BlockSpec(memory_space=pl.ANY)],
        out_specs=(vmem, vmem, vmem),
        scratch_shapes=[pltpu.VMEM((2, 16, HEAD), f32)],
        compiler_params=pltpu.CompilerParams(vmem_limit_bytes=8 << 20),
        name="weigh",
    )(ref_margin, pair_prompt, load, done)


def join_kernel(parts_ref, out_ref):
    total = parts_ref[0].astype(f32)
    for i in range(1, 64):
        total = total + parts_ref[i].astype(f32)
    out_ref[...] = jnp.broadcast_to(total.astype(bf16)[None], out_ref.shape)


def join(parts):
    vmem = pl.BlockSpec(memory_space=pltpu.VMEM)
    return pl.pallas_call(
        join_kernel,
        out_shape=jax.ShapeDtypeStruct((32, 8, HEAD), bf16),
        in_specs=[vmem],
        out_specs=vmem,
        compiler_params=pltpu.CompilerParams(vmem_limit_bytes=8 << 20),
        name="join",
    )(parts)


def to_all(pieces, axes):
    return lax.all_to_all(pieces, axes, 0, 0, tiled=True)


def copies_to_all(shard, axes):
    size = lax.axis_size(axes)
    return to_all(jnp.broadcast_to(shard[None], (size, *shard.shape)), axes)


def on_device(
    prompt_kv, response_queries, resp_kv, readout, slot_response, lengths, pair_prompt, ref_margin
):
    near = copies_to_all(prompt_kv, "z")
    place = lax.axis_index("c").astype(jnp.int32)[None]
    q, r, part = prepare(slot_response, lengths, response_queries, readout, resp_kv)
    near, q, r, part = lax.optimization_barrier((near, q, r, part))
    far = lax.ppermute(near, "c", [(0, 1), (1, 0)])
    stats, contrib = forward(slot_response, pair_prompt, q, r, part, near, far)
    contribs = to_all(contrib, APART)
    load = backward(slot_response, pair_prompt, place, q, r, stats, near, far)
    share = jnp.sum(contribs, axis=0)
    load = to_all(with_news(slot_response, share, load), CLOSE)
    dq, down, done = finish(slot_response, pair_prompt, q, r, stats, near, far, resp_kv)
    margins, weights, parts = weigh(
        ref_margin.reshape(4, HEAD), pair_prompt.reshape(4, HEAD), load, done
    )
    pairs = jnp.arange(ref_margin.shape[0])
    sign = 1.0 - 2.0 * (slot_response % 2).astype(f32)
    found = jnp.where((slot_response // 2)[:, None] == pairs, weights.reshape(1, -1), 0.0)
    own = (jnp.sum(found, axis=1) * sign)[:, None, None]
    grad_q = (own * dq.astype(f32)).astype(bf16)
    grad_own = (own * down.astype(f32)).astype(bf16)
    total = join(to_all(parts.reshape(64, 8, HEAD), APART))
    total = to_all(total, RESP).reshape(8, 4, 2, 4, HEAD)
    grad_prompt = jnp.transpose(total, (2, 0, 3, 1, 4)).reshape(2, 32, 512)
    return margins.reshape(-1), grad_q, grad_own, grad_prompt


def solution(mesh):
    split = Mesh(mesh.devices.reshape(8, 2, 8, 4), EVERY)
    in_specs = (
        P(None, PREFIX, None),
        P(EVERY, None, None),
        P(EVERY, None, None),
        P(EVERY, None, None),
        P(EVERY),
        P(),
        P(),
        P(),
    )
    out_specs = (P(), P(EVERY, None, None), P(EVERY, None, None), P(None, PREFIX, None))
    return jax.shard_map(
        on_device, mesh=split, in_specs=in_specs, out_specs=out_specs, check_vma=False
    )
```

```python
import math

import jax
import jax.numpy as jnp
from jax import lax
from jax.experimental import pallas as pl
from jax.experimental.pallas import tpu as pltpu
from jax.sharding import Mesh
from jax.sharding import PartitionSpec as P

QUERY_HEADS = 14
KEY_VALUE_HEADS = 2
HEAD = 128
GROUP = QUERY_HEADS // KEY_VALUE_HEADS
TOKENS = 128
WIDTH = GROUP * HEAD
KEYS = 640
SCALE = HEAD**-0.5
LOG2_SCALE = SCALE * math.log2(math.e)
MARGIN_BETA = 0.1
LOSS_SCALE = 256.0
EVERY = ("z", "c", "y", "x")
PREFIX = ("z", "c")
RESP = ("y", "x")
CLOSE = ("c", "x")
APART = ("z", "y")
LOAD_ROWS = 528
GRANT = 52
NT = (((1,), (1,)), ((), ()))
NN = (((1,), (0,)), ((), ()))
bf16 = jnp.bfloat16
f32 = jnp.float32


def pair_grid():
    ids = lax.broadcasted_iota(jnp.int32, (4, HEAD), 0) * HEAD
    return ids + lax.broadcasted_iota(jnp.int32, (4, HEAD), 1)


def fill(dest, near_ref, far_ref, prompt, column):
    at = pl.ds(pl.multiple_of(column, HEAD), HEAD)
    dest[0:256, :] = near_ref[:, prompt, :, at].reshape(256, HEAD)
    dest[256:512, :] = far_ref[:, prompt, :, at].reshape(256, HEAD)


def dots(keys, values, q, r):
    scores = lax.dot_general(keys, q, NT, preferred_element_type=f32)
    return scores, lax.dot_general(values, r, NT, preferred_element_type=f32)


def causal(scores):
    j = lax.broadcasted_iota(jnp.int32, (TOKENS, WIDTH), 0)
    t = lax.broadcasted_iota(jnp.int32, (TOKENS, WIDTH), 1) % TOKENS
    return jnp.where(j <= t, scores, -1e30)


def own_part(own_ref, group, is_value):
    column = (is_value * KEY_VALUE_HEADS + group) * HEAD
    return own_ref[0, :, pl.ds(pl.multiple_of(column, HEAD), HEAD)]


def prepare_kernel(
    response_ref, lengths_ref, q_ref, r_ref, own_ref, q_out, r_out, stats_ref
):
    group = pl.program_id(1)
    length = lengths_ref[response_ref[pl.program_id(0)]]
    live = lax.broadcasted_iota(jnp.int32, (TOKENS, HEAD), 0) < length
    for h in range(GROUP):
        rows = slice(h * TOKENS, (h + 1) * TOKENS)
        columns = slice(h * HEAD, (h + 1) * HEAD)
        q_out[0, rows, :] = q_ref[0, :, columns]
        r_out[0, rows, :] = jnp.where(live, r_ref[0, :, columns], jnp.zeros((), bf16))
    scores, dprobs = dots(
        own_part(own_ref, group, 0), own_part(own_ref, group, 1), q_out[0], r_out[0]
    )
    scores = causal(scores)
    top = jnp.max(scores, axis=0, keepdims=True)
    weight = jnp.exp2((scores - top) * LOG2_SCALE)
    stats_ref[0, 0:1, :] = top
    stats_ref[0, 1:2, :] = jnp.sum(weight, axis=0, keepdims=True)
    stats_ref[0, 2:3, :] = jnp.sum(weight * dprobs, axis=0, keepdims=True)


def forward_kernel(
    response_ref, pair_prompt_ref, q_ref, r_ref, part_ref, near_ref, far_ref,
    stats_ref, contrib_ref, key_s, value_s, sums_s,
):
    slot = pl.program_id(0)
    group = pl.program_id(1)
    prompt = pair_prompt_ref[response_ref[slot] // 2]
    fill(key_s, near_ref, far_ref, prompt, group * HEAD)
    fill(value_s, near_ref, far_ref, prompt, (KEY_VALUE_HEADS + group) * HEAD)
    top, total, delta = (part_ref[0, i : i + 1, :] for i in range(3))
    for start in range(0, 512, 128):
        keys = slice(start, start + 128)
        scores, dprobs = dots(key_s[keys, :], value_s[keys, :], q_ref[0], r_ref[0])
        higher = jnp.maximum(top, jnp.max(scores, axis=0, keepdims=True))
        weight = jnp.exp2((scores - higher) * LOG2_SCALE)
        fade = jnp.exp2((top - higher) * LOG2_SCALE)
        total = total * fade + jnp.sum(weight, axis=0, keepdims=True)
        delta = delta * fade + jnp.sum(weight * dprobs, axis=0, keepdims=True)
        top = higher
    share = 1.0 / total
    delta = delta * share
    stats_ref[0, 0:1, :] = top
    stats_ref[0, 1:2, :] = share
    stats_ref[0, 2:3, :] = delta
    total = jnp.sum(delta, axis=1, keepdims=True)

    @pl.when(group == 0)
    def _():
        sums_s[slot] = jnp.broadcast_to(total, (8, HEAD))

    @pl.when(group == 1)
    def _():
        sums_s[slot] = sums_s[slot] + total

    @pl.when((slot == 1) & (group == 1))
    def _():
        ids = pair_grid()
        contrib = jnp.zeros((4, HEAD), f32)
        for s in range(2):
            response = response_ref[s]
            sign = (1 - 2 * (response % 2)).astype(f32)
            contrib = contrib + jnp.where(ids == response // 2, sign * sums_s[s][0:4], 0.0)
        contrib_ref[...] = jnp.broadcast_to(contrib[None], contrib_ref.shape)


def backward_parts(scores, dprobs, stats_ref):
    top, share, delta = (stats_ref[0, i : i + 1, :] for i in range(3))
    probs = jnp.exp2((scores - top) * LOG2_SCALE) * share
    return probs.astype(bf16), (probs * (dprobs - delta)).astype(bf16)


def backward_kernel(
    response_ref, pair_prompt_ref, place_ref, q_ref, r_ref, stats_ref, near_ref, far_ref,
    load_ref, key_s, value_s, probs_s, dscores_s,
):
    slot = pl.program_id(0)
    group = pl.program_id(1)
    prompt = pair_prompt_ref[response_ref[slot] // 2]
    mine = place_ref[0]
    fill(key_s, near_ref, far_ref, prompt, group * HEAD)
    fill(value_s, near_ref, far_ref, prompt, (KEY_VALUE_HEADS + group) * HEAD)
    scores, dprobs = dots(key_s[...], value_s[...], q_ref[0], r_ref[0])
    probs_s[...], dscores_s[...] = backward_parts(scores, dprobs, stats_ref)
    dkey = lax.dot_general(dscores_s[...], q_ref[0], NN, preferred_element_type=f32) * SCALE
    dvalue = lax.dot_general(probs_s[...], r_ref[0], NN, preferred_element_type=f32)
    rows = pl.ds(pl.multiple_of(slot * 256, 256), 256)
    for i, grad in enumerate((dkey, dvalue)):
        grad = grad.astype(bf16)
        for core in range(2):
            dest = jnp.bitwise_xor(mine, core) * 4 + i * KEY_VALUE_HEADS + group
            load_ref[dest, rows, :] = grad[core * 256 : (core + 1) * 256]


def finish_kernel(
    response_ref, pair_prompt_ref, q_ref, r_ref, stats_ref, near_ref, far_ref, own_ref,
    dq_ref, down_ref, done_ref, key_s, value_s, probs_s, dscores_s,
):
    group = pl.program_id(1)
    prompt = pair_prompt_ref[response_ref[pl.program_id(0)] // 2]
    fill(key_s, near_ref, far_ref, prompt, group * HEAD)
    fill(value_s, near_ref, far_ref, prompt, (KEY_VALUE_HEADS + group) * HEAD)
    key_s[512:640, :] = own_part(own_ref, group, 0)
    value_s[512:640, :] = own_part(own_ref, group, 1)
    scores, dprobs = dots(key_s[...], value_s[...], q_ref[0], r_ref[0])
    scores = jnp.concatenate([scores[:512], causal(scores[512:])], axis=0)
    probs, dscores_s[...] = backward_parts(scores, dprobs, stats_ref)
    probs_s[...] = probs[512:]
    dq = lax.dot_general(key_s[...].T, dscores_s[...], NN, preferred_element_type=f32) * SCALE
    for h in range(GROUP):
        part = slice(h * HEAD, (h + 1) * HEAD)
        dq_ref[0, :, part] = dq[:, part].T.astype(bf16)
    dkey = lax.dot_general(dscores_s[512:640, :], q_ref[0], NN, preferred_element_type=f32)
    dvalue = lax.dot_general(probs_s[...], r_ref[0], NN, preferred_element_type=f32)
    column = pl.multiple_of(group * HEAD, HEAD)
    down_ref[0, :, pl.ds(column, HEAD)] = (dkey * SCALE).astype(bf16)
    column = pl.multiple_of((KEY_VALUE_HEADS + group) * HEAD, HEAD)
    down_ref[0, :, pl.ds(column, HEAD)] = dvalue.astype(bf16)
    done_ref[...] = jnp.zeros((8, HEAD), f32)


def whole(shape):
    return pl.BlockSpec(shape, lambda s, g, *_: (0,) * len(shape))


def by_slot(shape):
    return pl.BlockSpec(shape, lambda s, g, *_: (s, 0, 0))


def by_group(shape):
    return pl.BlockSpec(shape, lambda s, g, *_: (s, 0, g))


def by_both(shape):
    return pl.BlockSpec(shape, lambda s, g, *_: (s * 2 + g, 0, 0))


VMEM = pl.BlockSpec(memory_space=pltpu.VMEM)
STACK = by_both((1, WIDTH, HEAD))
STATS = by_both((1, 8, WIDTH))
STACK_SHAPE = jax.ShapeDtypeStruct((4, WIDTH, HEAD), bf16)
STATS_SHAPE = jax.ShapeDtypeStruct((4, 8, WIDTH), f32)


def per_group(kernel, name, scalars, arrays, in_specs, out_specs, out_shape, scratch, flops, exps):
    return pl.pallas_call(
        kernel,
        out_shape=out_shape,
        grid_spec=pltpu.PrefetchScalarGridSpec(
            num_scalar_prefetch=len(scalars),
            grid=(2, 2),
            in_specs=in_specs,
            out_specs=out_specs,
            scratch_shapes=scratch,
        ),
        compiler_params=pltpu.CompilerParams(vmem_limit_bytes=GRANT << 20),
        cost_estimate=pl.CostEstimate(
            flops=flops, bytes_accessed=4_000_000, transcendentals=exps
        ),
        name=name,
    )(*scalars, *arrays)


def prepare(slot_response, lengths, queries, readout, own):
    return per_group(
        prepare_kernel, "prepare",
        (slot_response, lengths), (queries, readout, own),
        [by_group((1, TOKENS, WIDTH)), by_group((1, TOKENS, WIDTH)), by_slot((1, TOKENS, 512))],
        [STACK, STACK, STATS],
        (STACK_SHAPE, STACK_SHAPE, STATS_SHAPE),
        [], 240_000_000, 460_000,
    )


def forward(slot_response, pair_prompt, q, r, part, near, far):
    return per_group(
        forward_kernel, "forward",
        (slot_response, pair_prompt), (q, r, part, near, far),
        [STACK, STACK, STATS, VMEM, VMEM],
        [STATS, whole((64, 4, HEAD))],
        (STATS_SHAPE, jax.ShapeDtypeStruct((64, 4, HEAD), f32)),
        [
            pltpu.VMEM((512, HEAD), bf16),
            pltpu.VMEM((512, HEAD), bf16),
            pltpu.VMEM((2, 8, HEAD), f32),
        ],
        940_000_000, 1_800_000,
    )


def backward(slot_response, pair_prompt, place, q, r, stats, near, far):
    return per_group(
        backward_kernel, "backward",
        (slot_response, pair_prompt, place), (q, r, stats, near, far),
        [STACK, STACK, STATS, VMEM, VMEM],
        whole((8, LOAD_ROWS, HEAD)),
        jax.ShapeDtypeStruct((8, LOAD_ROWS, HEAD), bf16),
        [
            pltpu.VMEM((512, HEAD), bf16),
            pltpu.VMEM((512, HEAD), bf16),
            pltpu.VMEM((512, WIDTH), bf16),
            pltpu.VMEM((512, WIDTH), bf16),
        ],
        1_880_000_000, 1_800_000,
    )


def finish(slot_response, pair_prompt, q, r, stats, near, far, own):
    return per_group(
        finish_kernel, "finish",
        (slot_response, pair_prompt), (q, r, stats, near, far, own),
        [STACK, STACK, STATS, VMEM, VMEM, by_slot((1, TOKENS, 512))],
        [by_group((1, TOKENS, WIDTH)), by_slot((1, TOKENS, 512)), whole((8, HEAD))],
        (
            jax.ShapeDtypeStruct((2, TOKENS, QUERY_HEADS * HEAD), bf16),
            jax.ShapeDtypeStruct((2, TOKENS, 512), bf16),
            jax.ShapeDtypeStruct((8, HEAD), f32),
        ),
        [
            pltpu.VMEM((KEYS, HEAD), bf16),
            pltpu.VMEM((KEYS, HEAD), bf16),
            pltpu.VMEM((TOKENS, WIDTH), bf16),
            pltpu.VMEM((KEYS, WIDTH), bf16),
        ],
        2_000_000_000, 2_300_000,
    )


def with_news(slot_response, share, load):
    high = lax.reduce_precision(share, 8, 7)
    middle = lax.reduce_precision(share - high, 8, 7)
    low = share - high - middle
    names = jnp.stack([slot_response // 32, slot_response % 32], axis=1).reshape(4, 1)
    names = jnp.broadcast_to(names.astype(f32), (4, HEAD))
    news = jnp.concatenate([high, middle, low, names], axis=0).astype(bf16)
    news = jnp.broadcast_to(news[None], (8, 16, HEAD))
    return lax.dynamic_update_slice(load, news, (0, 512, 0))


def weigh_kernel(
    ref_margin_ref, pair_prompt_ref, load_ref, done_ref, margins_ref, weights_ref, out_ref, factor_s
):
    del done_ref
    pair_sums = jnp.zeros((4, HEAD), f32)
    names = []
    for source in range(8):
        n = load_ref[source, 512:528, :].astype(f32)
        pair_sums = pair_sums + (n[0:4] + n[4:8] + n[8:12])
        names += [n[12:13] * 32.0 + n[13:14], n[14:15] * 32.0 + n[15:16]]
    margins = MARGIN_BETA * (pair_sums - ref_margin_ref[...])
    margins_ref[...] = margins
    weights = -LOSS_SCALE * MARGIN_BETA * jax.nn.sigmoid(-margins)
    weights_ref[...] = weights
    responses = jnp.concatenate(names, axis=0).astype(jnp.int32)
    sign = (1 - 2 * (responses % 2)).astype(f32)
    lane = lax.broadcasted_iota(jnp.int32, (16, HEAD), 1)
    for p in range(2):
        table = jnp.where(pair_prompt_ref[...] == p, weights, 0.0)
        found = jnp.zeros((16, HEAD), f32)
        for k in range(4):
            found = jnp.where(responses // 2 == lane + k * HEAD, table[k : k + 1], found)
        factor_s[p] = sign * jnp.sum(found, axis=1, keepdims=True)

    def step(z, _):
        sums = [jnp.zeros((32, HEAD), f32) for _ in range(2)]
        for source in range(8):
            for slot in range(2):
                rows = pl.ds(pl.multiple_of(slot * 256 + z * 32, 32), 32)
                piece = load_ref[source, rows, :].astype(f32)
                at = source * 2 + slot
                for p in range(2):
                    sums[p] = sums[p] + factor_s[p, at : at + 1, :] * piece
        for p in range(2):
            out_ref[z, p * 4 : p * 4 + 4] = sums[p].reshape(4, 8, HEAD).astype(bf16)
        return 0

    lax.fori_loop(0, 8, step, 0)


def weigh(ref_margin, pair_prompt, load, done):
    vmem = pl.BlockSpec(memory_space=pltpu.VMEM)
    return pl.pallas_call(
        weigh_kernel,
        out_shape=(
            jax.ShapeDtypeStruct((4, HEAD), f32),
            jax.ShapeDtypeStruct((4, HEAD), f32),
            jax.ShapeDtypeStruct((8, 8, 8, HEAD), bf16),
        ),
        in_specs=[vmem, vmem, vmem, pl.BlockSpec(memory_space=pl.ANY)],
        out_specs=(vmem, vmem, vmem),
        scratch_shapes=[pltpu.VMEM((2, 16, HEAD), f32)],
        compiler_params=pltpu.CompilerParams(vmem_limit_bytes=8 << 20),
        name="weigh",
    )(ref_margin, pair_prompt, load, done)


def join_kernel(parts_ref, out_ref):
    total = parts_ref[0].astype(f32)
    for i in range(1, 64):
        total = total + parts_ref[i].astype(f32)
    out_ref[...] = jnp.broadcast_to(total.astype(bf16)[None], out_ref.shape)


def join(parts):
    vmem = pl.BlockSpec(memory_space=pltpu.VMEM)
    return pl.pallas_call(
        join_kernel,
        out_shape=jax.ShapeDtypeStruct((32, 8, HEAD), bf16),
        in_specs=[vmem],
        out_specs=vmem,
        compiler_params=pltpu.CompilerParams(vmem_limit_bytes=8 << 20),
        name="join",
    )(parts)


def to_all(pieces, axes):
    return lax.all_to_all(pieces, axes, 0, 0, tiled=True)


def repeat_kernel(shard_ref, out_ref, sems):
    copies = [
        pltpu.make_async_copy(shard_ref, out_ref.at[i], sems.at[i])
        for i in range(out_ref.shape[0])
    ]
    for copy in copies:
        copy.start()
    for copy in copies:
        copy.wait()


def copies_to_all(shard, axes):
    size = lax.axis_size(axes)
    hbm = pl.BlockSpec(memory_space=pltpu.HBM)
    repeated = pl.pallas_call(
        repeat_kernel,
        out_shape=jax.ShapeDtypeStruct((size, *shard.shape), shard.dtype),
        in_specs=[hbm],
        out_specs=hbm,
        scratch_shapes=[pltpu.SemaphoreType.DMA((size,))],
        name="repeat",
    )(shard)
    return to_all(repeated, axes)


def on_device(
    prompt_kv, response_queries, resp_kv, readout, slot_response, lengths, pair_prompt, ref_margin
):
    near = copies_to_all(prompt_kv, "z")
    place = lax.axis_index("c").astype(jnp.int32)[None]
    q, r, part = prepare(slot_response, lengths, response_queries, readout, resp_kv)
    near, q, r, part = lax.optimization_barrier((near, q, r, part))
    far = lax.ppermute(near, "c", [(0, 1), (1, 0)])
    stats, contrib = forward(slot_response, pair_prompt, q, r, part, near, far)
    contribs = to_all(contrib, APART)
    load = backward(slot_response, pair_prompt, place, q, r, stats, near, far)
    share = jnp.sum(contribs, axis=0)
    load = to_all(with_news(slot_response, share, load), CLOSE)
    dq, down, done = finish(slot_response, pair_prompt, q, r, stats, near, far, resp_kv)
    margins, weights, parts = weigh(
        ref_margin.reshape(4, HEAD), pair_prompt.reshape(4, HEAD), load, done
    )
    pairs = jnp.arange(ref_margin.shape[0])
    sign = 1.0 - 2.0 * (slot_response % 2).astype(f32)
    found = jnp.where((slot_response // 2)[:, None] == pairs, weights.reshape(1, -1), 0.0)
    own = (jnp.sum(found, axis=1) * sign)[:, None, None]
    grad_q = (own * dq.astype(f32)).astype(bf16)
    grad_own = (own * down.astype(f32)).astype(bf16)
    total = join(to_all(parts.reshape(64, 8, HEAD), APART))
    total = to_all(total, RESP).reshape(2, 4, 4, 8, HEAD)
    grad_prompt = jnp.transpose(total, (0, 1, 3, 2, 4)).reshape(2, 32, 512)
    return margins.reshape(-1), grad_q, grad_own, grad_prompt


def solution(mesh):
    split = Mesh(mesh.devices.reshape(8, 2, 8, 4), EVERY)
    in_specs = (
        P(None, PREFIX, None),
        P(EVERY, None, None),
        P(EVERY, None, None),
        P(EVERY, None, None),
        P(EVERY),
        P(),
        P(),
        P(),
    )
    out_specs = (P(), P(EVERY, None, None), P(EVERY, None, None), P(None, PREFIX, None))
    return jax.shard_map(
        on_device, mesh=split, in_specs=in_specs, out_specs=out_specs, check_vma=False
    )
```

```python
import math

import jax
import jax.numpy as jnp
from jax import lax
from jax.experimental import pallas as pl
from jax.experimental.pallas import tpu as pltpu
from jax.sharding import Mesh
from jax.sharding import PartitionSpec as P

QUERY_HEADS = 14
KEY_VALUE_HEADS = 2
HEAD = 128
GROUP = QUERY_HEADS // KEY_VALUE_HEADS
TOKENS = 128
WIDTH = GROUP * HEAD
KEYS = 640
SCALE = HEAD**-0.5
LOG2_SCALE = SCALE * math.log2(math.e)
MARGIN_BETA = 0.1
LOSS_SCALE = 256.0
EVERY = ("z", "c", "y", "x")
PREFIX = ("z", "c")
RESP = ("y", "x")
APART = ("z", "y")
SHARERS = ("z", "c", "y")
HALF_ROWS = 528
LOAD_ROWS = 2 * HALF_ROWS + 16
GRANT = 52
NT = (((1,), (1,)), ((), ()))
NN = (((1,), (0,)), ((), ()))
bf16 = jnp.bfloat16
f32 = jnp.float32


def pair_grid():
    ids = lax.broadcasted_iota(jnp.int32, (4, HEAD), 0) * HEAD
    return ids + lax.broadcasted_iota(jnp.int32, (4, HEAD), 1)


def fill(dest, near_ref, far_ref, prompt, column):
    at = pl.ds(pl.multiple_of(column, HEAD), HEAD)
    dest[0:256, :] = near_ref[:, prompt, :, at].reshape(256, HEAD)
    dest[256:512, :] = far_ref[:, prompt, :, at].reshape(256, HEAD)


def dots(keys, values, q, r):
    scores = lax.dot_general(keys, q, NT, preferred_element_type=f32)
    return scores, lax.dot_general(values, r, NT, preferred_element_type=f32)


def causal(scores):
    j = lax.broadcasted_iota(jnp.int32, (TOKENS, WIDTH), 0)
    t = lax.broadcasted_iota(jnp.int32, (TOKENS, WIDTH), 1) % TOKENS
    return jnp.where(j <= t, scores, -1e30)


def own_part(own_ref, group, is_value):
    column = (is_value * KEY_VALUE_HEADS + group) * HEAD
    return own_ref[0, :, pl.ds(pl.multiple_of(column, HEAD), HEAD)]


def prepare_kernel(
    response_ref, lengths_ref, q_ref, r_ref, own_ref, q_out, r_out, stats_ref
):
    group = pl.program_id(1)
    length = lengths_ref[response_ref[pl.program_id(0)]]
    live = lax.broadcasted_iota(jnp.int32, (TOKENS, HEAD), 0) < length
    for h in range(GROUP):
        rows = slice(h * TOKENS, (h + 1) * TOKENS)
        columns = slice(h * HEAD, (h + 1) * HEAD)
        q_out[0, rows, :] = q_ref[0, :, columns]
        r_out[0, rows, :] = jnp.where(live, r_ref[0, :, columns], jnp.zeros((), bf16))
    scores, dprobs = dots(
        own_part(own_ref, group, 0), own_part(own_ref, group, 1), q_out[0], r_out[0]
    )
    scores = causal(scores)
    top = jnp.max(scores, axis=0, keepdims=True)
    weight = jnp.exp2((scores - top) * LOG2_SCALE)
    stats_ref[0, 0:1, :] = top
    stats_ref[0, 1:2, :] = jnp.sum(weight, axis=0, keepdims=True)
    stats_ref[0, 2:3, :] = jnp.sum(weight * dprobs, axis=0, keepdims=True)


def forward_kernel(
    response_ref, pair_prompt_ref, q_ref, r_ref, part_ref, near_ref, far_ref,
    stats_ref, contrib_ref, key_s, value_s, sums_s,
):
    slot = pl.program_id(0)
    group = pl.program_id(1)
    prompt = pair_prompt_ref[response_ref[slot] // 2]
    fill(key_s, near_ref, far_ref, prompt, group * HEAD)
    fill(value_s, near_ref, far_ref, prompt, (KEY_VALUE_HEADS + group) * HEAD)
    top, total, delta = (part_ref[0, i : i + 1, :] for i in range(3))
    for start in range(0, 512, 128):
        keys = slice(start, start + 128)
        scores, dprobs = dots(key_s[keys, :], value_s[keys, :], q_ref[0], r_ref[0])
        higher = jnp.maximum(top, jnp.max(scores, axis=0, keepdims=True))
        weight = jnp.exp2((scores - higher) * LOG2_SCALE)
        fade = jnp.exp2((top - higher) * LOG2_SCALE)
        total = total * fade + jnp.sum(weight, axis=0, keepdims=True)
        delta = delta * fade + jnp.sum(weight * dprobs, axis=0, keepdims=True)
        top = higher
    share = 1.0 / total
    delta = delta * share
    stats_ref[0, 0:1, :] = top
    stats_ref[0, 1:2, :] = share
    stats_ref[0, 2:3, :] = delta
    total = jnp.sum(delta, axis=1, keepdims=True)

    @pl.when(group == 0)
    def _():
        sums_s[slot] = jnp.broadcast_to(total, (8, HEAD))

    @pl.when(group == 1)
    def _():
        sums_s[slot] = sums_s[slot] + total

    @pl.when((slot == 1) & (group == 1))
    def _():
        ids = pair_grid()
        contrib = jnp.zeros((4, HEAD), f32)
        for s in range(2):
            response = response_ref[s]
            sign = (1 - 2 * (response % 2)).astype(f32)
            contrib = contrib + jnp.where(ids == response // 2, sign * sums_s[s][0:4], 0.0)
        contrib_ref[...] = jnp.broadcast_to(contrib[None], contrib_ref.shape)


def backward_parts(scores, dprobs, stats_ref):
    top, share, delta = (stats_ref[0, i : i + 1, :] for i in range(3))
    probs = jnp.exp2((scores - top) * LOG2_SCALE) * share
    return probs.astype(bf16), (probs * (dprobs - delta)).astype(bf16)


def backward_kernel(
    response_ref, pair_prompt_ref, q_ref, r_ref, stats_ref, near_ref, far_ref,
    load_ref, other_ref, key_s, value_s, probs_s, dscores_s,
):
    slot = pl.program_id(0)
    group = pl.program_id(1)
    prompt = pair_prompt_ref[response_ref[slot] // 2]
    fill(key_s, near_ref, far_ref, prompt, group * HEAD)
    fill(value_s, near_ref, far_ref, prompt, (KEY_VALUE_HEADS + group) * HEAD)
    scores, dprobs = dots(key_s[...], value_s[...], q_ref[0], r_ref[0])
    probs_s[...], dscores_s[...] = backward_parts(scores, dprobs, stats_ref)
    dkey = lax.dot_general(dscores_s[...], q_ref[0], NN, preferred_element_type=f32) * SCALE
    dvalue = lax.dot_general(probs_s[...], r_ref[0], NN, preferred_element_type=f32)
    rows = pl.ds(pl.multiple_of(slot * 256, 256), 256)
    for i, grad in enumerate((dkey, dvalue)):
        grad = grad.astype(bf16)
        dest = i * KEY_VALUE_HEADS + group
        load_ref[dest, rows, :] = grad[:256]
        other_ref[dest, rows, :] = grad[256:]

    @pl.when((slot == 0) & (group == 0))
    def _():
        row = lax.broadcasted_iota(jnp.int32, (16, HEAD), 0)
        names = jnp.zeros((16, HEAD), f32)
        for s in range(2):
            response = response_ref[s]
            names = jnp.where(row == 2 * s, (response // 32).astype(f32), names)
            names = jnp.where(row == 2 * s + 1, (response % 32).astype(f32), names)
        for dest in range(4):
            load_ref[dest, 512:528, :] = names.astype(bf16)
            other_ref[dest, 512:528, :] = names.astype(bf16)


def finish_kernel(
    response_ref, pair_prompt_ref, q_ref, r_ref, stats_ref, near_ref, far_ref, own_ref,
    dq_ref, down_ref, done_ref, key_s, value_s, probs_s, dscores_s,
):
    group = pl.program_id(1)
    prompt = pair_prompt_ref[response_ref[pl.program_id(0)] // 2]
    fill(key_s, near_ref, far_ref, prompt, group * HEAD)
    fill(value_s, near_ref, far_ref, prompt, (KEY_VALUE_HEADS + group) * HEAD)
    key_s[512:640, :] = own_part(own_ref, group, 0)
    value_s[512:640, :] = own_part(own_ref, group, 1)
    scores, dprobs = dots(key_s[...], value_s[...], q_ref[0], r_ref[0])
    scores = jnp.concatenate([scores[:512], causal(scores[512:])], axis=0)
    probs, dscores_s[...] = backward_parts(scores, dprobs, stats_ref)
    probs_s[...] = probs[512:]
    dq = lax.dot_general(key_s[...].T, dscores_s[...], NN, preferred_element_type=f32) * SCALE
    for h in range(GROUP):
        part = slice(h * HEAD, (h + 1) * HEAD)
        dq_ref[0, :, part] = dq[:, part].T.astype(bf16)
    dkey = lax.dot_general(dscores_s[512:640, :], q_ref[0], NN, preferred_element_type=f32)
    dvalue = lax.dot_general(probs_s[...], r_ref[0], NN, preferred_element_type=f32)
    column = pl.multiple_of(group * HEAD, HEAD)
    down_ref[0, :, pl.ds(column, HEAD)] = (dkey * SCALE).astype(bf16)
    column = pl.multiple_of((KEY_VALUE_HEADS + group) * HEAD, HEAD)
    down_ref[0, :, pl.ds(column, HEAD)] = dvalue.astype(bf16)
    done_ref[...] = jnp.zeros((8, HEAD), f32)


def whole(shape):
    return pl.BlockSpec(shape, lambda s, g, *_: (0,) * len(shape))


def by_slot(shape):
    return pl.BlockSpec(shape, lambda s, g, *_: (s, 0, 0))


def by_group(shape):
    return pl.BlockSpec(shape, lambda s, g, *_: (s, 0, g))


def by_both(shape):
    return pl.BlockSpec(shape, lambda s, g, *_: (s * 2 + g, 0, 0))


VMEM = pl.BlockSpec(memory_space=pltpu.VMEM)
STACK = by_both((1, WIDTH, HEAD))
STATS = by_both((1, 8, WIDTH))
STACK_SHAPE = jax.ShapeDtypeStruct((4, WIDTH, HEAD), bf16)
STATS_SHAPE = jax.ShapeDtypeStruct((4, 8, WIDTH), f32)


def per_group(kernel, name, scalars, arrays, in_specs, out_specs, out_shape, scratch, flops, exps):
    return pl.pallas_call(
        kernel,
        out_shape=out_shape,
        grid_spec=pltpu.PrefetchScalarGridSpec(
            num_scalar_prefetch=len(scalars),
            grid=(2, 2),
            in_specs=in_specs,
            out_specs=out_specs,
            scratch_shapes=scratch,
        ),
        compiler_params=pltpu.CompilerParams(vmem_limit_bytes=GRANT << 20),
        cost_estimate=pl.CostEstimate(
            flops=flops, bytes_accessed=4_000_000, transcendentals=exps
        ),
        name=name,
    )(*scalars, *arrays)


def prepare(slot_response, lengths, queries, readout, own):
    return per_group(
        prepare_kernel, "prepare",
        (slot_response, lengths), (queries, readout, own),
        [by_group((1, TOKENS, WIDTH)), by_group((1, TOKENS, WIDTH)), by_slot((1, TOKENS, 512))],
        [STACK, STACK, STATS],
        (STACK_SHAPE, STACK_SHAPE, STATS_SHAPE),
        [], 240_000_000, 460_000,
    )


def forward(slot_response, pair_prompt, q, r, part, near, far):
    return per_group(
        forward_kernel, "forward",
        (slot_response, pair_prompt), (q, r, part, near, far),
        [STACK, STACK, STATS, VMEM, VMEM],
        [STATS, whole((128, 4, HEAD))],
        (STATS_SHAPE, jax.ShapeDtypeStruct((128, 4, HEAD), f32)),
        [
            pltpu.VMEM((512, HEAD), bf16),
            pltpu.VMEM((512, HEAD), bf16),
            pltpu.VMEM((2, 8, HEAD), f32),
        ],
        940_000_000, 1_800_000,
    )


def backward(slot_response, pair_prompt, q, r, stats, near, far):
    return per_group(
        backward_kernel, "backward",
        (slot_response, pair_prompt), (q, r, stats, near, far),
        [STACK, STACK, STATS, VMEM, VMEM],
        [whole((4, LOAD_ROWS, HEAD)), whole((4, HALF_ROWS, HEAD))],
        (
            jax.ShapeDtypeStruct((4, LOAD_ROWS, HEAD), bf16),
            jax.ShapeDtypeStruct((4, HALF_ROWS, HEAD), bf16),
        ),
        [
            pltpu.VMEM((512, HEAD), bf16),
            pltpu.VMEM((512, HEAD), bf16),
            pltpu.VMEM((512, WIDTH), bf16),
            pltpu.VMEM((512, WIDTH), bf16),
        ],
        1_880_000_000, 1_800_000,
    )


def finish(slot_response, pair_prompt, q, r, stats, near, far, own):
    return per_group(
        finish_kernel, "finish",
        (slot_response, pair_prompt), (q, r, stats, near, far, own),
        [STACK, STACK, STATS, VMEM, VMEM, by_slot((1, TOKENS, 512))],
        [by_group((1, TOKENS, WIDTH)), by_slot((1, TOKENS, 512)), whole((8, HEAD))],
        (
            jax.ShapeDtypeStruct((2, TOKENS, QUERY_HEADS * HEAD), bf16),
            jax.ShapeDtypeStruct((2, TOKENS, 512), bf16),
            jax.ShapeDtypeStruct((8, HEAD), f32),
        ),
        [
            pltpu.VMEM((KEYS, HEAD), bf16),
            pltpu.VMEM((KEYS, HEAD), bf16),
            pltpu.VMEM((TOKENS, WIDTH), bf16),
            pltpu.VMEM((KEYS, WIDTH), bf16),
        ],
        2_000_000_000, 2_300_000,
    )


def with_news(share, load):
    high = lax.reduce_precision(share, 8, 7)
    middle = lax.reduce_precision(share - high, 8, 7)
    low = share - high - middle
    news = jnp.concatenate([high, middle, low, jnp.zeros_like(low)], axis=0).astype(bf16)
    news = jnp.broadcast_to(news[None], (4, 16, HEAD))
    return lax.dynamic_update_slice(load, news, (0, 2 * HALF_ROWS, 0))


def weigh_kernel(
    ref_margin_ref, pair_prompt_ref, load_ref, done_ref, margins_ref, weights_ref, out_ref, factor_s
):
    del done_ref
    pair_sums = jnp.zeros((4, HEAD), f32)
    names = []
    for source in range(4):
        n = load_ref[source, 2 * HALF_ROWS : LOAD_ROWS, :].astype(f32)
        pair_sums = pair_sums + (n[0:4] + n[4:8] + n[8:12])
        for core in range(2):
            n = load_ref[source, core * HALF_ROWS + 512 : (core + 1) * HALF_ROWS, :].astype(f32)
            names += [n[0:1] * 32.0 + n[1:2], n[2:3] * 32.0 + n[3:4]]
    margins = MARGIN_BETA * (pair_sums - ref_margin_ref[...])
    margins_ref[...] = margins
    weights = -LOSS_SCALE * MARGIN_BETA * jax.nn.sigmoid(-margins)
    weights_ref[...] = weights
    responses = jnp.concatenate(names, axis=0).astype(jnp.int32)
    sign = (1 - 2 * (responses % 2)).astype(f32)
    lane = lax.broadcasted_iota(jnp.int32, (16, HEAD), 1)
    for p in range(2):
        table = jnp.where(pair_prompt_ref[...] == p, weights, 0.0)
        found = jnp.zeros((16, HEAD), f32)
        for k in range(4):
            found = jnp.where(responses // 2 == lane + k * HEAD, table[k : k + 1], found)
        factor_s[p] = sign * jnp.sum(found, axis=1, keepdims=True)

    def step(z, _):
        sums = [jnp.zeros((32, HEAD), f32) for _ in range(2)]
        for source in range(4):
            for at in range(4):
                base = at // 2 * HALF_ROWS + at % 2 * 256
                rows = pl.ds(pl.multiple_of(base + z * 32, 16), 32)
                piece = load_ref[source, rows, :].astype(f32)
                for p in range(2):
                    which = source * 4 + at
                    sums[p] = sums[p] + factor_s[p, which : which + 1, :] * piece
        for p in range(2):
            out_ref[z, p * 4 : p * 4 + 4] = sums[p].reshape(4, 8, HEAD).astype(bf16)
        return 0

    lax.fori_loop(0, 8, step, 0)


def weigh(ref_margin, pair_prompt, load, done):
    vmem = pl.BlockSpec(memory_space=pltpu.VMEM)
    return pl.pallas_call(
        weigh_kernel,
        out_shape=(
            jax.ShapeDtypeStruct((4, HEAD), f32),
            jax.ShapeDtypeStruct((4, HEAD), f32),
            jax.ShapeDtypeStruct((8, 8, 8, HEAD), bf16),
        ),
        in_specs=[vmem, vmem, vmem, pl.BlockSpec(memory_space=pl.ANY)],
        out_specs=(vmem, vmem, vmem),
        scratch_shapes=[pltpu.VMEM((2, 16, HEAD), f32)],
        compiler_params=pltpu.CompilerParams(vmem_limit_bytes=8 << 20),
        name="weigh",
    )(ref_margin, pair_prompt, load, done)


def join_kernel(parts_ref, out_ref):
    total = parts_ref[0].astype(f32)
    for i in range(1, 64):
        total = total + parts_ref[i].astype(f32)
    out_ref[...] = jnp.broadcast_to(total.astype(bf16)[None], out_ref.shape)


def join(parts):
    vmem = pl.BlockSpec(memory_space=pltpu.VMEM)
    return pl.pallas_call(
        join_kernel,
        out_shape=jax.ShapeDtypeStruct((32, 8, HEAD), bf16),
        in_specs=[vmem],
        out_specs=vmem,
        compiler_params=pltpu.CompilerParams(vmem_limit_bytes=8 << 20),
        name="join",
    )(parts)


def to_all(pieces, axes):
    return lax.all_to_all(pieces, axes, 0, 0, tiled=True)


def copies_to_all(shard, axes):
    size = lax.axis_size(axes)
    return to_all(jnp.broadcast_to(shard[None], (size, *shard.shape)), axes)


def on_device(
    prompt_kv, response_queries, resp_kv, readout, slot_response, lengths, pair_prompt, ref_margin
):
    near = copies_to_all(prompt_kv, "z")
    q, r, part = prepare(slot_response, lengths, response_queries, readout, resp_kv)
    near, q, r, part = lax.optimization_barrier((near, q, r, part))
    far = lax.ppermute(near, "c", [(0, 1), (1, 0)])
    stats, contrib = forward(slot_response, pair_prompt, q, r, part, near, far)
    contribs = to_all(contrib, SHARERS)
    load, other = backward(slot_response, pair_prompt, q, r, stats, near, far)
    got = lax.ppermute(other, "c", [(0, 1), (1, 0)])
    load = lax.dynamic_update_slice(load, got, (0, HALF_ROWS, 0))
    contribs, load = lax.optimization_barrier((contribs, load))
    share = jnp.sum(contribs, axis=0)
    load = to_all(with_news(share, load), "x")
    dq, down, done = finish(slot_response, pair_prompt, q, r, stats, near, far, resp_kv)
    margins, weights, parts = weigh(
        ref_margin.reshape(4, HEAD), pair_prompt.reshape(4, HEAD), load, done
    )
    pairs = jnp.arange(ref_margin.shape[0])
    sign = 1.0 - 2.0 * (slot_response % 2).astype(f32)
    found = jnp.where((slot_response // 2)[:, None] == pairs, weights.reshape(1, -1), 0.0)
    own = (jnp.sum(found, axis=1) * sign)[:, None, None]
    grad_q = (own * dq.astype(f32)).astype(bf16)
    grad_own = (own * down.astype(f32)).astype(bf16)
    total = join(to_all(parts.reshape(64, 8, HEAD), APART))
    total = to_all(total, RESP).reshape(2, 4, 4, 8, HEAD)
    grad_prompt = jnp.transpose(total, (0, 1, 3, 2, 4)).reshape(2, 32, 512)
    return margins.reshape(-1), grad_q, grad_own, grad_prompt


def solution(mesh):
    split = Mesh(mesh.devices.reshape(8, 2, 8, 4), EVERY)
    in_specs = (
        P(None, PREFIX, None),
        P(EVERY, None, None),
        P(EVERY, None, None),
        P(EVERY, None, None),
        P(EVERY),
        P(),
        P(),
        P(),
    )
    out_specs = (P(), P(EVERY, None, None), P(EVERY, None, None), P(None, PREFIX, None))
    return jax.shard_map(
        on_device, mesh=split, in_specs=in_specs, out_specs=out_specs, check_vma=False
    )
```

```python
import math

import jax
import jax.numpy as jnp
from jax import lax
from jax.experimental import pallas as pl
from jax.experimental.pallas import tpu as pltpu
from jax.sharding import Mesh
from jax.sharding import PartitionSpec as P

QUERY_HEADS = 14
KEY_VALUE_HEADS = 2
HEAD = 128
GROUP = QUERY_HEADS // KEY_VALUE_HEADS
TOKENS = 128
WIDTH = GROUP * HEAD
KEYS = 640
SCALE = HEAD**-0.5
LOG2_SCALE = SCALE * math.log2(math.e)
MARGIN_BETA = 0.1
LOSS_SCALE = 256.0
EVERY = ("z", "c", "y", "x")
PREFIX = ("z", "c")
RESP = ("y", "x")
CLOSE = ("c", "x")
APART = ("z", "y")
LOAD_ROWS = 528
GRANT = 52
NT = (((1,), (1,)), ((), ()))
NN = (((1,), (0,)), ((), ()))
bf16 = jnp.bfloat16
f32 = jnp.float32


def pair_grid():
    ids = lax.broadcasted_iota(jnp.int32, (4, HEAD), 0) * HEAD
    return ids + lax.broadcasted_iota(jnp.int32, (4, HEAD), 1)


def fill(dest, near_ref, far_ref, prompt, column):
    at = pl.ds(pl.multiple_of(column, HEAD), HEAD)
    dest[0:256, :] = near_ref[:, prompt, :, at].reshape(256, HEAD)
    dest[256:512, :] = far_ref[:, prompt, :, at].reshape(256, HEAD)


def dots(keys, values, q, r):
    scores = lax.dot_general(keys, q, NT, preferred_element_type=f32)
    return scores, lax.dot_general(values, r, NT, preferred_element_type=f32)


def causal(scores):
    j = lax.broadcasted_iota(jnp.int32, (TOKENS, WIDTH), 0)
    t = lax.broadcasted_iota(jnp.int32, (TOKENS, WIDTH), 1) % TOKENS
    return jnp.where(j <= t, scores, -1e30)


def own_part(own_ref, group, is_value):
    column = (is_value * KEY_VALUE_HEADS + group) * HEAD
    return own_ref[0, :, pl.ds(pl.multiple_of(column, HEAD), HEAD)]


def prepare_kernel(
    response_ref, lengths_ref, q_ref, r_ref, own_ref, q_out, r_out, stats_ref
):
    group = pl.program_id(1)
    length = lengths_ref[response_ref[pl.program_id(0)]]
    live = lax.broadcasted_iota(jnp.int32, (TOKENS, HEAD), 0) < length
    for h in range(GROUP):
        rows = slice(h * TOKENS, (h + 1) * TOKENS)
        columns = slice(h * HEAD, (h + 1) * HEAD)
        q_out[0, rows, :] = q_ref[0, :, columns]
        r_out[0, rows, :] = jnp.where(live, r_ref[0, :, columns], jnp.zeros((), bf16))
    scores, dprobs = dots(
        own_part(own_ref, group, 0), own_part(own_ref, group, 1), q_out[0], r_out[0]
    )
    scores = causal(scores)
    top = jnp.max(scores, axis=0, keepdims=True)
    weight = jnp.exp2((scores - top) * LOG2_SCALE)
    stats_ref[0, 0:1, :] = top
    stats_ref[0, 1:2, :] = jnp.sum(weight, axis=0, keepdims=True)
    stats_ref[0, 2:3, :] = jnp.sum(weight * dprobs, axis=0, keepdims=True)


def forward_kernel(
    response_ref, pair_prompt_ref, q_ref, r_ref, part_ref, near_ref, far_ref,
    stats_ref, contrib_ref, key_s, value_s, sums_s,
):
    slot = pl.program_id(0)
    group = pl.program_id(1)
    prompt = pair_prompt_ref[response_ref[slot] // 2]
    fill(key_s, near_ref, far_ref, prompt, group * HEAD)
    fill(value_s, near_ref, far_ref, prompt, (KEY_VALUE_HEADS + group) * HEAD)
    top, total, delta = (part_ref[0, i : i + 1, :] for i in range(3))
    for start in range(0, 512, 128):
        keys = slice(start, start + 128)
        scores, dprobs = dots(key_s[keys, :], value_s[keys, :], q_ref[0], r_ref[0])
        higher = jnp.maximum(top, jnp.max(scores, axis=0, keepdims=True))
        weight = jnp.exp2((scores - higher) * LOG2_SCALE)
        fade = jnp.exp2((top - higher) * LOG2_SCALE)
        total = total * fade + jnp.sum(weight, axis=0, keepdims=True)
        delta = delta * fade + jnp.sum(weight * dprobs, axis=0, keepdims=True)
        top = higher
    share = 1.0 / total
    delta = delta * share
    stats_ref[0, 0:1, :] = top
    stats_ref[0, 1:2, :] = share
    stats_ref[0, 2:3, :] = delta
    total = jnp.sum(delta, axis=1, keepdims=True)

    @pl.when(group == 0)
    def _():
        sums_s[slot] = jnp.broadcast_to(total, (8, HEAD))

    @pl.when(group == 1)
    def _():
        sums_s[slot] = sums_s[slot] + total

    @pl.when((slot == 1) & (group == 1))
    def _():
        ids = pair_grid()
        contrib = jnp.zeros((4, HEAD), f32)
        for s in range(2):
            response = response_ref[s]
            sign = (1 - 2 * (response % 2)).astype(f32)
            contrib = contrib + jnp.where(ids == response // 2, sign * sums_s[s][0:4], 0.0)
        contrib_ref[...] = jnp.broadcast_to(contrib[None], contrib_ref.shape)


def backward_parts(scores, dprobs, stats_ref):
    top, share, delta = (stats_ref[0, i : i + 1, :] for i in range(3))
    probs = jnp.exp2((scores - top) * LOG2_SCALE) * share
    return probs.astype(bf16), (probs * (dprobs - delta)).astype(bf16)


def backward_kernel(
    response_ref, pair_prompt_ref, place_ref, q_ref, r_ref, stats_ref, near_ref, far_ref,
    load_ref, key_s, value_s, probs_s, dscores_s,
):
    slot = pl.program_id(0)
    group = pl.program_id(1)
    prompt = pair_prompt_ref[response_ref[slot] // 2]
    mine = place_ref[0]
    fill(key_s, near_ref, far_ref, prompt, group * HEAD)
    fill(value_s, near_ref, far_ref, prompt, (KEY_VALUE_HEADS + group) * HEAD)
    scores, dprobs = dots(key_s[...], value_s[...], q_ref[0], r_ref[0])
    probs_s[...], dscores_s[...] = backward_parts(scores, dprobs, stats_ref)
    dkey = lax.dot_general(dscores_s[...], q_ref[0], NN, preferred_element_type=f32) * SCALE
    dvalue = lax.dot_general(probs_s[...], r_ref[0], NN, preferred_element_type=f32)
    rows = pl.ds(pl.multiple_of(slot * 256, 256), 256)
    for i, grad in enumerate((dkey, dvalue)):
        grad = grad.astype(bf16)
        for core in range(2):
            dest = jnp.bitwise_xor(mine, core) * 4 + i * KEY_VALUE_HEADS + group
            load_ref[dest, rows, :] = grad[core * 256 : (core + 1) * 256]


def finish_kernel(
    response_ref, pair_prompt_ref, q_ref, r_ref, stats_ref, near_ref, far_ref, own_ref,
    dq_ref, down_ref, done_ref, key_s, value_s, probs_s, dscores_s,
):
    group = pl.program_id(1)
    prompt = pair_prompt_ref[response_ref[pl.program_id(0)] // 2]
    fill(key_s, near_ref, far_ref, prompt, group * HEAD)
    fill(value_s, near_ref, far_ref, prompt, (KEY_VALUE_HEADS + group) * HEAD)
    key_s[512:640, :] = own_part(own_ref, group, 0)
    value_s[512:640, :] = own_part(own_ref, group, 1)
    scores, dprobs = dots(key_s[...], value_s[...], q_ref[0], r_ref[0])
    scores = jnp.concatenate([scores[:512], causal(scores[512:])], axis=0)
    probs, dscores_s[...] = backward_parts(scores, dprobs, stats_ref)
    probs_s[...] = probs[512:]
    dq = lax.dot_general(key_s[...].T, dscores_s[...], NN, preferred_element_type=f32) * SCALE
    for h in range(GROUP):
        part = slice(h * HEAD, (h + 1) * HEAD)
        dq_ref[0, :, part] = dq[:, part].T.astype(bf16)
    dkey = lax.dot_general(dscores_s[512:640, :], q_ref[0], NN, preferred_element_type=f32)
    dvalue = lax.dot_general(probs_s[...], r_ref[0], NN, preferred_element_type=f32)
    column = pl.multiple_of(group * HEAD, HEAD)
    down_ref[0, :, pl.ds(column, HEAD)] = (dkey * SCALE).astype(bf16)
    column = pl.multiple_of((KEY_VALUE_HEADS + group) * HEAD, HEAD)
    down_ref[0, :, pl.ds(column, HEAD)] = dvalue.astype(bf16)
    done_ref[...] = jnp.zeros((8, HEAD), f32)


def whole(shape):
    return pl.BlockSpec(shape, lambda s, g, *_: (0,) * len(shape))


def by_slot(shape):
    return pl.BlockSpec(shape, lambda s, g, *_: (s, 0, 0))


def by_group(shape):
    return pl.BlockSpec(shape, lambda s, g, *_: (s, 0, g))


def by_both(shape):
    return pl.BlockSpec(shape, lambda s, g, *_: (s * 2 + g, 0, 0))


VMEM = pl.BlockSpec(memory_space=pltpu.VMEM)
STACK = by_both((1, WIDTH, HEAD))
STATS = by_both((1, 8, WIDTH))
STACK_SHAPE = jax.ShapeDtypeStruct((4, WIDTH, HEAD), bf16)
STATS_SHAPE = jax.ShapeDtypeStruct((4, 8, WIDTH), f32)


def per_group(kernel, name, scalars, arrays, in_specs, out_specs, out_shape, scratch, flops, exps):
    return pl.pallas_call(
        kernel,
        out_shape=out_shape,
        grid_spec=pltpu.PrefetchScalarGridSpec(
            num_scalar_prefetch=len(scalars),
            grid=(2, 2),
            in_specs=in_specs,
            out_specs=out_specs,
            scratch_shapes=scratch,
        ),
        compiler_params=pltpu.CompilerParams(vmem_limit_bytes=GRANT << 20),
        cost_estimate=pl.CostEstimate(
            flops=flops, bytes_accessed=4_000_000, transcendentals=exps
        ),
        name=name,
    )(*scalars, *arrays)


def prepare(slot_response, lengths, queries, readout, own):
    return per_group(
        prepare_kernel, "prepare",
        (slot_response, lengths), (queries, readout, own),
        [by_group((1, TOKENS, WIDTH)), by_group((1, TOKENS, WIDTH)), by_slot((1, TOKENS, 512))],
        [STACK, STACK, STATS],
        (STACK_SHAPE, STACK_SHAPE, STATS_SHAPE),
        [], 240_000_000, 460_000,
    )


def forward(slot_response, pair_prompt, q, r, part, near, far):
    return per_group(
        forward_kernel, "forward",
        (slot_response, pair_prompt), (q, r, part, near, far),
        [STACK, STACK, STATS, VMEM, VMEM],
        [STATS, whole((64, 4, HEAD))],
        (STATS_SHAPE, jax.ShapeDtypeStruct((64, 4, HEAD), f32)),
        [
            pltpu.VMEM((512, HEAD), bf16),
            pltpu.VMEM((512, HEAD), bf16),
            pltpu.VMEM((2, 8, HEAD), f32),
        ],
        940_000_000, 1_800_000,
    )


def backward(slot_response, pair_prompt, place, q, r, stats, near, far):
    return per_group(
        backward_kernel, "backward",
        (slot_response, pair_prompt, place), (q, r, stats, near, far),
        [STACK, STACK, STATS, VMEM, VMEM],
        whole((8, LOAD_ROWS, HEAD)),
        jax.ShapeDtypeStruct((8, LOAD_ROWS, HEAD), bf16),
        [
            pltpu.VMEM((512, HEAD), bf16),
            pltpu.VMEM((512, HEAD), bf16),
            pltpu.VMEM((512, WIDTH), bf16),
            pltpu.VMEM((512, WIDTH), bf16),
        ],
        1_880_000_000, 1_800_000,
    )


def finish(slot_response, pair_prompt, q, r, stats, near, far, own):
    return per_group(
        finish_kernel, "finish",
        (slot_response, pair_prompt), (q, r, stats, near, far, own),
        [STACK, STACK, STATS, VMEM, VMEM, by_slot((1, TOKENS, 512))],
        [by_group((1, TOKENS, WIDTH)), by_slot((1, TOKENS, 512)), whole((8, HEAD))],
        (
            jax.ShapeDtypeStruct((2, TOKENS, QUERY_HEADS * HEAD), bf16),
            jax.ShapeDtypeStruct((2, TOKENS, 512), bf16),
            jax.ShapeDtypeStruct((8, HEAD), f32),
        ),
        [
            pltpu.VMEM((KEYS, HEAD), bf16),
            pltpu.VMEM((KEYS, HEAD), bf16),
            pltpu.VMEM((TOKENS, WIDTH), bf16),
            pltpu.VMEM((KEYS, WIDTH), bf16),
        ],
        2_000_000_000, 2_300_000,
    )


def with_news(slot_response, share, load):
    high = lax.reduce_precision(share, 8, 7)
    middle = lax.reduce_precision(share - high, 8, 7)
    low = share - high - middle
    names = jnp.stack([slot_response // 32, slot_response % 32], axis=1).reshape(4, 1)
    names = jnp.broadcast_to(names.astype(f32), (4, HEAD))
    news = jnp.concatenate([high, middle, low, names], axis=0).astype(bf16)
    news = jnp.broadcast_to(news[None], (8, 16, HEAD))
    return lax.dynamic_update_slice(load, news, (0, 512, 0))


def weigh_kernel(
    ref_margin_ref, pair_prompt_ref, load_ref, done_ref, margins_ref, weights_ref, out_ref, factor_s
):
    del done_ref
    pair_sums = jnp.zeros((4, HEAD), f32)
    names = []
    for source in range(8):
        n = load_ref[source, 512:528, :].astype(f32)
        pair_sums = pair_sums + (n[0:4] + n[4:8] + n[8:12])
        names += [n[12:13] * 32.0 + n[13:14], n[14:15] * 32.0 + n[15:16]]
    margins = MARGIN_BETA * (pair_sums - ref_margin_ref[...])
    margins_ref[...] = margins
    weights = -LOSS_SCALE * MARGIN_BETA * jax.nn.sigmoid(-margins)
    weights_ref[...] = weights
    responses = jnp.concatenate(names, axis=0).astype(jnp.int32)
    sign = (1 - 2 * (responses % 2)).astype(f32)
    lane = lax.broadcasted_iota(jnp.int32, (16, HEAD), 1)
    for p in range(2):
        table = jnp.where(pair_prompt_ref[...] == p, weights, 0.0)
        found = jnp.zeros((16, HEAD), f32)
        for k in range(4):
            found = jnp.where(responses // 2 == lane + k * HEAD, table[k : k + 1], found)
        factor_s[p] = sign * jnp.sum(found, axis=1, keepdims=True)

    def step(z, _):
        sums = [jnp.zeros((32, HEAD), f32) for _ in range(2)]
        for source in range(8):
            for slot in range(2):
                rows = pl.ds(pl.multiple_of(slot * 256 + z * 32, 32), 32)
                piece = load_ref[source, rows, :].astype(f32)
                at = source * 2 + slot
                for p in range(2):
                    sums[p] = sums[p] + factor_s[p, at : at + 1, :] * piece
        for p in range(2):
            out_ref[z, p * 4 : p * 4 + 4] = sums[p].reshape(4, 8, HEAD).astype(bf16)
        return 0

    lax.fori_loop(0, 8, step, 0)


def weigh(ref_margin, pair_prompt, load, done):
    vmem = pl.BlockSpec(memory_space=pltpu.VMEM)
    return pl.pallas_call(
        weigh_kernel,
        out_shape=(
            jax.ShapeDtypeStruct((4, HEAD), f32),
            jax.ShapeDtypeStruct((4, HEAD), f32),
            jax.ShapeDtypeStruct((8, 8, 8, HEAD), bf16),
        ),
        in_specs=[vmem, vmem, vmem, pl.BlockSpec(memory_space=pl.ANY)],
        out_specs=(vmem, vmem, vmem),
        scratch_shapes=[pltpu.VMEM((2, 16, HEAD), f32)],
        compiler_params=pltpu.CompilerParams(vmem_limit_bytes=8 << 20),
        name="weigh",
    )(ref_margin, pair_prompt, load, done)


def join_kernel(parts_ref, out_ref):
    total = parts_ref[0].astype(f32)
    for i in range(1, 64):
        total = total + parts_ref[i].astype(f32)
    out_ref[...] = jnp.broadcast_to(total.astype(bf16)[None], out_ref.shape)


def join(parts):
    vmem = pl.BlockSpec(memory_space=pltpu.VMEM)
    return pl.pallas_call(
        join_kernel,
        out_shape=jax.ShapeDtypeStruct((32, 8, HEAD), bf16),
        in_specs=[vmem],
        out_specs=vmem,
        compiler_params=pltpu.CompilerParams(vmem_limit_bytes=8 << 20),
        name="join",
    )(parts)


def to_all(pieces, axes):
    return lax.all_to_all(pieces, axes, 0, 0, tiled=True)


def copies_to_all(shard, axes):
    size = lax.axis_size(axes)
    return to_all(jnp.broadcast_to(shard[None], (size, *shard.shape)), axes)


def on_device(
    prompt_kv, response_queries, resp_kv, readout, slot_response, lengths, pair_prompt, ref_margin
):
    near = copies_to_all(prompt_kv, "z")
    place = lax.axis_index("c").astype(jnp.int32)[None]
    q, r, part = prepare(slot_response, lengths, response_queries, readout, resp_kv)
    near, q, r, part = lax.optimization_barrier((near, q, r, part))
    far = lax.ppermute(near, "c", [(0, 1), (1, 0)])
    stats, contrib = forward(slot_response, pair_prompt, q, r, part, near, far)
    contribs = to_all(contrib, APART)
    load = backward(slot_response, pair_prompt, place, q, r, stats, near, far)
    share = jnp.sum(contribs, axis=0)
    load = to_all(with_news(slot_response, share, load), CLOSE)
    dq, down, done = finish(slot_response, pair_prompt, q, r, stats, near, far, resp_kv)
    margins, weights, parts = weigh(
        ref_margin.reshape(4, HEAD), pair_prompt.reshape(4, HEAD), load, done
    )
    pairs = jnp.arange(ref_margin.shape[0])
    sign = 1.0 - 2.0 * (slot_response % 2).astype(f32)
    found = jnp.where((slot_response // 2)[:, None] == pairs, weights.reshape(1, -1), 0.0)
    own = (jnp.sum(found, axis=1) * sign)[:, None, None]
    grad_q = (own * dq.astype(f32)).astype(bf16)
    grad_own = (own * down.astype(f32)).astype(bf16)
    total = join(to_all(parts.reshape(64, 8, HEAD), APART))
    total = to_all(total, RESP).reshape(2, 4, 4, 8, HEAD)
    grad_prompt = jnp.transpose(total, (0, 1, 3, 2, 4)).reshape(2, 32, 512)
    return margins.reshape(-1), grad_q, grad_own, grad_prompt


def solution(mesh):
    split = Mesh(mesh.devices.reshape(8, 2, 8, 4), EVERY)
    in_specs = (
        P(None, PREFIX, None),
        P(EVERY, None, None),
        P(EVERY, None, None),
        P(EVERY, None, None),
        P(EVERY),
        P(),
        P(),
        P(),
    )
    out_specs = (P(), P(EVERY, None, None), P(EVERY, None, None), P(None, PREFIX, None))
    return jax.shard_map(
        on_device, mesh=split, in_specs=in_specs, out_specs=out_specs, check_vma=False
    )
```

```python
import math

import jax
import jax.numpy as jnp
from jax import lax
from jax.experimental import pallas as pl
from jax.experimental.pallas import tpu as pltpu
from jax.sharding import Mesh
from jax.sharding import PartitionSpec as P

QUERY_HEADS = 14
KEY_VALUE_HEADS = 2
HEAD = 128
GROUP = QUERY_HEADS // KEY_VALUE_HEADS
TOKENS = 128
WIDTH = GROUP * HEAD
KEYS = 640
SCALE = HEAD**-0.5
LOG2_SCALE = SCALE * math.log2(math.e)
MARGIN_BETA = 0.1
LOSS_SCALE = 256.0
EVERY = ("z", "c", "y", "x")
PREFIX = ("z", "c")
RESP = ("y", "x")
CLOSE = ("c", "x")
APART = ("z", "y")
LOAD_ROWS = 528
GRANT = 52
NT = (((1,), (1,)), ((), ()))
NN = (((1,), (0,)), ((), ()))
bf16 = jnp.bfloat16
f32 = jnp.float32


def pair_grid():
    ids = lax.broadcasted_iota(jnp.int32, (4, HEAD), 0) * HEAD
    return ids + lax.broadcasted_iota(jnp.int32, (4, HEAD), 1)


def fill(dest, near_ref, far_ref, prompt, column):
    at = pl.ds(pl.multiple_of(column, HEAD), HEAD)
    dest[0:256, :] = near_ref[:, prompt, :, at].reshape(256, HEAD)
    dest[256:512, :] = far_ref[:, prompt, :, at].reshape(256, HEAD)


def dots(keys, values, q, r):
    scores = lax.dot_general(keys, q, NT, preferred_element_type=f32)
    return scores, lax.dot_general(values, r, NT, preferred_element_type=f32)


def causal(scores):
    j = lax.broadcasted_iota(jnp.int32, (TOKENS, WIDTH), 0)
    t = lax.broadcasted_iota(jnp.int32, (TOKENS, WIDTH), 1) % TOKENS
    return jnp.where(j <= t, scores, -1e30)


def own_part(own_ref, group, is_value):
    column = (is_value * KEY_VALUE_HEADS + group) * HEAD
    return own_ref[0, :, pl.ds(pl.multiple_of(column, HEAD), HEAD)]


def prepare_kernel(
    response_ref, lengths_ref, q_ref, r_ref, own_ref, q_out, r_out, stats_ref
):
    group = pl.program_id(1)
    length = lengths_ref[response_ref[pl.program_id(0)]]
    live = lax.broadcasted_iota(jnp.int32, (TOKENS, HEAD), 0) < length
    for h in range(GROUP):
        rows = slice(h * TOKENS, (h + 1) * TOKENS)
        columns = slice(h * HEAD, (h + 1) * HEAD)
        q_out[0, rows, :] = q_ref[0, :, columns]
        r_out[0, rows, :] = jnp.where(live, r_ref[0, :, columns], jnp.zeros((), bf16))
    scores, dprobs = dots(
        own_part(own_ref, group, 0), own_part(own_ref, group, 1), q_out[0], r_out[0]
    )
    scores = causal(scores)
    top = jnp.max(scores, axis=0, keepdims=True)
    weight = jnp.exp2((scores - top) * LOG2_SCALE)
    stats_ref[0, 0:1, :] = top
    stats_ref[0, 1:2, :] = jnp.sum(weight, axis=0, keepdims=True)
    stats_ref[0, 2:3, :] = jnp.sum(weight * dprobs, axis=0, keepdims=True)


def forward_kernel(
    response_ref, pair_prompt_ref, q_ref, r_ref, part_ref, near_ref, far_ref,
    stats_ref, contrib_ref, key_s, value_s, sums_s,
):
    slot = pl.program_id(0)
    group = pl.program_id(1)
    prompt = pair_prompt_ref[response_ref[slot] // 2]
    fill(key_s, near_ref, far_ref, prompt, group * HEAD)
    fill(value_s, near_ref, far_ref, prompt, (KEY_VALUE_HEADS + group) * HEAD)
    top, total, delta = (part_ref[0, i : i + 1, :] for i in range(3))
    for start in range(0, 512, 128):
        keys = slice(start, start + 128)
        scores, dprobs = dots(key_s[keys, :], value_s[keys, :], q_ref[0], r_ref[0])
        higher = jnp.maximum(top, jnp.max(scores, axis=0, keepdims=True))
        weight = jnp.exp2((scores - higher) * LOG2_SCALE)
        fade = jnp.exp2((top - higher) * LOG2_SCALE)
        total = total * fade + jnp.sum(weight, axis=0, keepdims=True)
        delta = delta * fade + jnp.sum(weight * dprobs, axis=0, keepdims=True)
        top = higher
    share = 1.0 / total
    delta = delta * share
    stats_ref[0, 0:1, :] = top
    stats_ref[0, 1:2, :] = share
    stats_ref[0, 2:3, :] = delta
    total = jnp.sum(delta, axis=1, keepdims=True)

    @pl.when(group == 0)
    def _():
        sums_s[slot] = jnp.broadcast_to(total, (8, HEAD))

    @pl.when(group == 1)
    def _():
        sums_s[slot] = sums_s[slot] + total

    @pl.when((slot == 1) & (group == 1))
    def _():
        ids = pair_grid()
        contrib = jnp.zeros((4, HEAD), f32)
        for s in range(2):
            response = response_ref[s]
            sign = (1 - 2 * (response % 2)).astype(f32)
            contrib = contrib + jnp.where(ids == response // 2, sign * sums_s[s][0:4], 0.0)
        contrib_ref[...] = jnp.broadcast_to(contrib[None], contrib_ref.shape)


def backward_parts(scores, dprobs, stats_ref):
    top, share, delta = (stats_ref[0, i : i + 1, :] for i in range(3))
    probs = jnp.exp2((scores - top) * LOG2_SCALE) * share
    return probs.astype(bf16), (probs * (dprobs - delta)).astype(bf16)


def backward_kernel(
    response_ref, pair_prompt_ref, place_ref, q_ref, r_ref, stats_ref, near_ref, far_ref,
    load_ref, key_s, value_s, probs_s, dscores_s,
):
    slot = pl.program_id(0)
    group = pl.program_id(1)
    prompt = pair_prompt_ref[response_ref[slot] // 2]
    mine = place_ref[0]
    fill(key_s, near_ref, far_ref, prompt, group * HEAD)
    fill(value_s, near_ref, far_ref, prompt, (KEY_VALUE_HEADS + group) * HEAD)
    scores, dprobs = dots(key_s[...], value_s[...], q_ref[0], r_ref[0])
    probs_s[...], dscores_s[...] = backward_parts(scores, dprobs, stats_ref)
    dkey = lax.dot_general(dscores_s[...], q_ref[0], NN, preferred_element_type=f32) * SCALE
    dvalue = lax.dot_general(probs_s[...], r_ref[0], NN, preferred_element_type=f32)
    rows = pl.ds(pl.multiple_of(slot * 256, 256), 256)
    for i, grad in enumerate((dkey, dvalue)):
        grad = grad.astype(bf16)
        for core in range(2):
            dest = jnp.bitwise_xor(mine, core) * 4 + i * KEY_VALUE_HEADS + group
            load_ref[dest, rows, :] = grad[core * 256 : (core + 1) * 256]


def finish_kernel(
    response_ref, pair_prompt_ref, q_ref, r_ref, stats_ref, near_ref, far_ref, own_ref,
    dq_ref, down_ref, done_ref, key_s, value_s, probs_s, dscores_s,
):
    group = pl.program_id(1)
    prompt = pair_prompt_ref[response_ref[pl.program_id(0)] // 2]
    fill(key_s, near_ref, far_ref, prompt, group * HEAD)
    fill(value_s, near_ref, far_ref, prompt, (KEY_VALUE_HEADS + group) * HEAD)
    key_s[512:640, :] = own_part(own_ref, group, 0)
    value_s[512:640, :] = own_part(own_ref, group, 1)
    scores, dprobs = dots(key_s[...], value_s[...], q_ref[0], r_ref[0])
    scores = jnp.concatenate([scores[:512], causal(scores[512:])], axis=0)
    probs, dscores_s[...] = backward_parts(scores, dprobs, stats_ref)
    probs_s[...] = probs[512:]
    dq = lax.dot_general(key_s[...].T, dscores_s[...], NN, preferred_element_type=f32) * SCALE
    for h in range(GROUP):
        part = slice(h * HEAD, (h + 1) * HEAD)
        dq_ref[0, :, part] = dq[:, part].T.astype(bf16)
    dkey = lax.dot_general(dscores_s[512:640, :], q_ref[0], NN, preferred_element_type=f32)
    dvalue = lax.dot_general(probs_s[...], r_ref[0], NN, preferred_element_type=f32)
    column = pl.multiple_of(group * HEAD, HEAD)
    down_ref[0, :, pl.ds(column, HEAD)] = (dkey * SCALE).astype(bf16)
    column = pl.multiple_of((KEY_VALUE_HEADS + group) * HEAD, HEAD)
    down_ref[0, :, pl.ds(column, HEAD)] = dvalue.astype(bf16)
    done_ref[...] = jnp.zeros((8, HEAD), f32)


def whole(shape):
    return pl.BlockSpec(shape, lambda s, g, *_: (0,) * len(shape))


def by_slot(shape):
    return pl.BlockSpec(shape, lambda s, g, *_: (s, 0, 0))


def by_group(shape):
    return pl.BlockSpec(shape, lambda s, g, *_: (s, 0, g))


def by_both(shape):
    return pl.BlockSpec(shape, lambda s, g, *_: (s * 2 + g, 0, 0))


VMEM = pl.BlockSpec(memory_space=pltpu.VMEM)
STACK = by_both((1, WIDTH, HEAD))
STATS = by_both((1, 8, WIDTH))
STACK_SHAPE = jax.ShapeDtypeStruct((4, WIDTH, HEAD), bf16)
STATS_SHAPE = jax.ShapeDtypeStruct((4, 8, WIDTH), f32)


def per_group(kernel, name, scalars, arrays, in_specs, out_specs, out_shape, scratch, flops, exps):
    return pl.pallas_call(
        kernel,
        out_shape=out_shape,
        grid_spec=pltpu.PrefetchScalarGridSpec(
            num_scalar_prefetch=len(scalars),
            grid=(2, 2),
            in_specs=in_specs,
            out_specs=out_specs,
            scratch_shapes=scratch,
        ),
        compiler_params=pltpu.CompilerParams(vmem_limit_bytes=GRANT << 20),
        cost_estimate=pl.CostEstimate(
            flops=flops, bytes_accessed=4_000_000, transcendentals=exps
        ),
        name=name,
    )(*scalars, *arrays)


def prepare(slot_response, lengths, queries, readout, own):
    return per_group(
        prepare_kernel, "prepare",
        (slot_response, lengths), (queries, readout, own),
        [by_group((1, TOKENS, WIDTH)), by_group((1, TOKENS, WIDTH)), by_slot((1, TOKENS, 512))],
        [STACK, STACK, STATS],
        (STACK_SHAPE, STACK_SHAPE, STATS_SHAPE),
        [], 240_000_000, 460_000,
    )


def forward(slot_response, pair_prompt, q, r, part, near, far):
    return per_group(
        forward_kernel, "forward",
        (slot_response, pair_prompt), (q, r, part, near, far),
        [STACK, STACK, STATS, VMEM, VMEM],
        [STATS, whole((64, 4, HEAD))],
        (STATS_SHAPE, jax.ShapeDtypeStruct((64, 4, HEAD), f32)),
        [
            pltpu.VMEM((512, HEAD), bf16),
            pltpu.VMEM((512, HEAD), bf16),
            pltpu.VMEM((2, 8, HEAD), f32),
        ],
        940_000_000, 1_800_000,
    )


def backward(slot_response, pair_prompt, place, q, r, stats, near, far):
    return per_group(
        backward_kernel, "backward",
        (slot_response, pair_prompt, place), (q, r, stats, near, far),
        [STACK, STACK, STATS, VMEM, VMEM],
        whole((8, LOAD_ROWS, HEAD)),
        jax.ShapeDtypeStruct((8, LOAD_ROWS, HEAD), bf16),
        [
            pltpu.VMEM((512, HEAD), bf16),
            pltpu.VMEM((512, HEAD), bf16),
            pltpu.VMEM((512, WIDTH), bf16),
            pltpu.VMEM((512, WIDTH), bf16),
        ],
        1_880_000_000, 1_800_000,
    )


def finish(slot_response, pair_prompt, q, r, stats, near, far, own):
    return per_group(
        finish_kernel, "finish",
        (slot_response, pair_prompt), (q, r, stats, near, far, own),
        [STACK, STACK, STATS, VMEM, VMEM, by_slot((1, TOKENS, 512))],
        [by_group((1, TOKENS, WIDTH)), by_slot((1, TOKENS, 512)), whole((8, HEAD))],
        (
            jax.ShapeDtypeStruct((2, TOKENS, QUERY_HEADS * HEAD), bf16),
            jax.ShapeDtypeStruct((2, TOKENS, 512), bf16),
            jax.ShapeDtypeStruct((8, HEAD), f32),
        ),
        [
            pltpu.VMEM((KEYS, HEAD), bf16),
            pltpu.VMEM((KEYS, HEAD), bf16),
            pltpu.VMEM((TOKENS, WIDTH), bf16),
            pltpu.VMEM((KEYS, WIDTH), bf16),
        ],
        2_000_000_000, 2_300_000,
    )


def with_news(slot_response, share, load):
    high = lax.reduce_precision(share, 8, 7)
    middle = lax.reduce_precision(share - high, 8, 7)
    low = share - high - middle
    names = jnp.stack([slot_response // 32, slot_response % 32], axis=1).reshape(4, 1)
    names = jnp.broadcast_to(names.astype(f32), (4, HEAD))
    news = jnp.concatenate([high, middle, low, names], axis=0).astype(bf16)
    news = jnp.broadcast_to(news[None], (8, 16, HEAD))
    return lax.dynamic_update_slice(load, news, (0, 512, 0))


def weigh_kernel(
    ref_margin_ref, pair_prompt_ref, load_ref, done_ref, margins_ref, weights_ref, out_ref, factor_s
):
    del done_ref
    pair_sums = jnp.zeros((4, HEAD), f32)
    names = []
    for source in range(8):
        n = load_ref[source, 512:528, :].astype(f32)
        pair_sums = pair_sums + (n[0:4] + n[4:8] + n[8:12])
        names += [n[12:13] * 32.0 + n[13:14], n[14:15] * 32.0 + n[15:16]]
    margins = MARGIN_BETA * (pair_sums - ref_margin_ref[...])
    margins_ref[...] = margins
    weights = -LOSS_SCALE * MARGIN_BETA * jax.nn.sigmoid(-margins)
    weights_ref[...] = weights
    responses = jnp.concatenate(names, axis=0).astype(jnp.int32)
    sign = (1 - 2 * (responses % 2)).astype(f32)
    lane = lax.broadcasted_iota(jnp.int32, (16, HEAD), 1)
    for p in range(2):
        table = jnp.where(pair_prompt_ref[...] == p, weights, 0.0)
        found = jnp.zeros((16, HEAD), f32)
        for k in range(4):
            found = jnp.where(responses // 2 == lane + k * HEAD, table[k : k + 1], found)
        factor_s[p] = sign * jnp.sum(found, axis=1, keepdims=True)

    def step(z, _):
        sums = [jnp.zeros((32, HEAD), f32) for _ in range(2)]
        for source in range(8):
            for slot in range(2):
                rows = pl.ds(pl.multiple_of(slot * 256 + z * 32, 32), 32)
                piece = load_ref[source, rows, :].astype(f32)
                at = source * 2 + slot
                for p in range(2):
                    sums[p] = sums[p] + factor_s[p, at : at + 1, :] * piece
        for p in range(2):
            out_ref[z, p * 4 : p * 4 + 4] = sums[p].reshape(4, 8, HEAD).astype(bf16)
        return 0

    lax.fori_loop(0, 8, step, 0)


def weigh(ref_margin, pair_prompt, load, done):
    vmem = pl.BlockSpec(memory_space=pltpu.VMEM)
    return pl.pallas_call(
        weigh_kernel,
        out_shape=(
            jax.ShapeDtypeStruct((4, HEAD), f32),
            jax.ShapeDtypeStruct((4, HEAD), f32),
            jax.ShapeDtypeStruct((8, 8, 8, HEAD), bf16),
        ),
        in_specs=[vmem, vmem, vmem, pl.BlockSpec(memory_space=pl.ANY)],
        out_specs=(vmem, vmem, vmem),
        scratch_shapes=[pltpu.VMEM((2, 16, HEAD), f32)],
        compiler_params=pltpu.CompilerParams(vmem_limit_bytes=8 << 20),
        name="weigh",
    )(ref_margin, pair_prompt, load, done)


def join_kernel(parts_ref, out_ref):
    total = parts_ref[0].astype(f32)
    for i in range(1, 64):
        total = total + parts_ref[i].astype(f32)
    out_ref[...] = jnp.broadcast_to(total.astype(bf16)[None], out_ref.shape)


def join(parts):
    vmem = pl.BlockSpec(memory_space=pltpu.VMEM)
    return pl.pallas_call(
        join_kernel,
        out_shape=jax.ShapeDtypeStruct((32, 8, HEAD), bf16),
        in_specs=[vmem],
        out_specs=vmem,
        compiler_params=pltpu.CompilerParams(vmem_limit_bytes=8 << 20),
        name="join",
    )(parts)


def to_all(pieces, axes):
    return lax.all_to_all(pieces, axes, 0, 0, tiled=True)


def repeat_kernel(shard_ref, out_ref, sems):
    copies = [
        pltpu.make_async_copy(shard_ref, out_ref.at[i], sems.at[i])
        for i in range(out_ref.shape[0])
    ]
    for copy in copies:
        copy.start()
    for copy in copies:
        copy.wait()


def copies_to_all(shard, axes):
    size = lax.axis_size(axes)
    repeated = pl.pallas_call(
        repeat_kernel,
        out_shape=jax.ShapeDtypeStruct((size, *shard.shape), shard.dtype),
        in_specs=[pl.BlockSpec(memory_space=pltpu.VMEM)],
        out_specs=pl.BlockSpec(memory_space=pltpu.HBM),
        scratch_shapes=[pltpu.SemaphoreType.DMA((size,))],
        compiler_params=pltpu.CompilerParams(vmem_limit_bytes=58 << 20),
        name="repeat",
    )(shard)
    return to_all(repeated, axes)


def on_device(
    prompt_kv, response_queries, resp_kv, readout, slot_response, lengths, pair_prompt, ref_margin
):
    near = copies_to_all(prompt_kv, "z")
    place = lax.axis_index("c").astype(jnp.int32)[None]
    q, r, part = prepare(slot_response, lengths, response_queries, readout, resp_kv)
    near, q, r, part = lax.optimization_barrier((near, q, r, part))
    far = lax.ppermute(near, "c", [(0, 1), (1, 0)])
    stats, contrib = forward(slot_response, pair_prompt, q, r, part, near, far)
    contribs = to_all(contrib, APART)
    load = backward(slot_response, pair_prompt, place, q, r, stats, near, far)
    share = jnp.sum(contribs, axis=0)
    load = to_all(with_news(slot_response, share, load), CLOSE)
    dq, down, done = finish(slot_response, pair_prompt, q, r, stats, near, far, resp_kv)
    margins, weights, parts = weigh(
        ref_margin.reshape(4, HEAD), pair_prompt.reshape(4, HEAD), load, done
    )
    pairs = jnp.arange(ref_margin.shape[0])
    sign = 1.0 - 2.0 * (slot_response % 2).astype(f32)
    found = jnp.where((slot_response // 2)[:, None] == pairs, weights.reshape(1, -1), 0.0)
    own = (jnp.sum(found, axis=1) * sign)[:, None, None]
    grad_q = (own * dq.astype(f32)).astype(bf16)
    grad_own = (own * down.astype(f32)).astype(bf16)
    total = join(to_all(parts.reshape(64, 8, HEAD), APART))
    total = to_all(total, RESP).reshape(2, 4, 4, 8, HEAD)
    grad_prompt = jnp.transpose(total, (0, 1, 3, 2, 4)).reshape(2, 32, 512)
    return margins.reshape(-1), grad_q, grad_own, grad_prompt


def solution(mesh):
    split = Mesh(mesh.devices.reshape(8, 2, 8, 4), EVERY)
    in_specs = (
        P(None, PREFIX, None),
        P(EVERY, None, None),
        P(EVERY, None, None),
        P(EVERY, None, None),
        P(EVERY),
        P(),
        P(),
        P(),
    )
    out_specs = (P(), P(EVERY, None, None), P(EVERY, None, None), P(None, PREFIX, None))
    return jax.shard_map(
        on_device, mesh=split, in_specs=in_specs, out_specs=out_specs, check_vma=False
    )
```
